32 devices in a mesh: fsdp: 16 (over z, y, core), tp: 2 (over x).
Axes of the slice: x: 2, y: 2, z: 4, core: 2. Of those that a mesh axis runs over, the one named last changes fastest.
Arguments:
- layer_input: bfloat16 [16, 512, 2048], P('fsdp', 'tp'), may hold values from -6 to 6
- attention_gain: float32 [2048], replicated, may hold values from 0.1 to 1.9
- query_gain: float32 [128], replicated, may hold values from 0.5 to 2
- key_gain: float32 [128], replicated, may hold values from 0.5 to 2
- query_weight: bfloat16 [2048, 4096], P('fsdp', 'tp'), may hold values from -0.125 to 0.125
- key_weight: bfloat16 [2048, 512], P('fsdp', 'tp'), may hold values from -0.125 to 0.125
- value_weight: bfloat16 [2048, 512], P('fsdp', 'tp'), may hold values from -0.125 to 0.125
- output_weight: bfloat16 [2048, 4096], P('fsdp', 'tp'), may hold values from -0.5 to 0.5
- router_weight: bfloat16 [2048, 32], P('fsdp'), may hold values from -0.125 to 0.125
- expert_gain: float32 [2048], replicated, may hold values from 0.1 to 1.9
- gate_weight: bfloat16 [32, 2048, 768], P('fsdp', None, 'tp'), may hold values from -0.125 to 0.125
- up_weight: bfloat16 [32, 2048, 768], P('fsdp', None, 'tp'), may hold values from -0.125 to 0.125
- down_weight: bfloat16 [32, 768, 2048], P('fsdp', 'tp'), may hold values from -0.625 to 0.625
- routes: int32 [16, 512, 8], P('fsdp'), may hold values from 0 to 31, all different within a row; in each aligned block of 512 rows (0 to 511, 512 to 1023, ..., all dimensions but the last counted through in order) at most 160 rows name the same one
- segments: int32 [16, 512], P('fsdp'), may hold values from 0 to 3, never falling along the last dimension, each value on 1 to 256 neighbouring positions
- cotangent: bfloat16 [16, 512, 2048], P('fsdp', 'tp'), may hold values from -6 to 6
Outputs:
- layer_output: bfloat16 [16, 512, 2048], P('fsdp', 'tp')
- input_grad: float32 [16, 512, 2048], P('fsdp', 'tp')
- attention_gain_grad: float32 [2048], P(('fsdp', 'tp'))
- query_gain_grad: float32 [128], P(('fsdp', 'tp'))
- key_gain_grad: float32 [128], P(('fsdp', 'tp'))
- query_grad: float32 [2048, 4096], P('fsdp', 'tp')
- key_grad: float32 [2048, 512], P('fsdp', 'tp')
- value_grad: float32 [2048, 512], P('fsdp', 'tp')
- output_grad: float32 [2048, 4096], P('fsdp', 'tp')
- router_grad: float32 [2048, 32], P(('fsdp', 'tp'))
- expert_gain_grad: float32 [2048], P(('fsdp', 'tp'))
- gate_grad: float32 [32, 2048, 768], P('fsdp', None, 'tp')
- up_grad: float32 [32, 2048, 768], P('fsdp', None, 'tp')
- down_grad: float32 [32, 768, 2048], P('fsdp', 'tp')
The draws below stay inside these ranges and needn't reach their ends.
Inputs may be any that keep to these rules, and one draw needn't show every extreme that they name: `routes`: each token names 8 different experts. Among the tokens of one group of 1 row no expert is named more than 160 times, and in some group one expert is named exactly 160 times. `segments`: within a row the numbers never fall; each segment spans 1 to 256 positions and some segment spans exactly that many.
All inputs are finite; a program needn't handle non-finite values.
Results may differ from the reference program's by a relative error of at most 0.022.
Values may be sent and summed in bfloat16 or wider, within the bound.
No kernel may reach another device: no remote copies, remote signals or barrier semaphores. Data moves between devices by JAX's collectives and lax.ppermute only.
A program may use at most 448 MiB of HBM per device.

```python
import math
import jax
import jax.numpy as jnp
import numpy as np
from jax import lax

D = 2048
H = 32
KVH = 4
HD = 128
FFE = 768
TOPK = 8
SEQ = 512
ROWS_DEV = 1
ROWS = 16
EXPERTS = 32
CAP = 160
N_FSDP = 16
N_TP = 2


def shard_levels(key, shape, cuts, least, largest):
    def one(dim, shards_of):
        draws = jax.random.uniform(jax.random.fold_in(jax.random.fold_in(key, 6), dim), (shards_of,), jnp.float32, least / len(cuts), largest / len(cuts))
        return jnp.repeat(jnp.exp(draws), shape[dim] // shards_of).reshape((-1,) + (1,) * (len(shape) - dim - 1))

    loudness = one(*cuts[0])
    for cut in cuts[1:]:
        loudness = loudness * one(*cut)
    return loudness


def split_up(amount, total, reach, slope):
    portions = [(1 << 20) // math.isqrt(grade ** slope) + 1 for grade in range(2, amount + 1)]
    surplus, counts = total - reach - (amount - 1), [1] * (amount - 1)
    while surplus > 0:
        candidates = [i for i in range(amount - 1) if counts[i] < reach]
        pool, left = sum([portions[i] for i in candidates]), surplus
        for i in candidates:
            addition = min(reach - counts[i], max(1, left * portions[i] // pool), surplus)
            counts[i] = counts[i] + addition
            surplus = surplus - addition
    return np.array([reach] + counts)


def ragged(rng, amount, total, limit, slope):
    if amount == 2:
        one = jax.random.randint(rng, (), max(1, total - limit), min(limit, total - 1) + 1)
        return jnp.stack([one, total - one])
    sizes = jnp.asarray(split_up(amount, total, limit, slope), jnp.int32)
    twos = (amount - 1) // 2
    source_of, taker = sizes[1:1 + 2 * twos:2], sizes[2:2 + 2 * twos:2]
    margin = jnp.minimum(source_of - 1, limit - taker)
    moved = jax.random.randint(jax.random.fold_in(rng, 1), (twos,), 0, 1 << 20) % (margin + 1)
    sizes = sizes.at[1:1 + 2 * twos:2].set(source_of - moved).at[2:2 + 2 * twos:2].set(taker + moved)
    return sizes[jax.random.permutation(jax.random.fold_in(rng, 2), amount)]


def routed_block(stream_key, own, number, rows, count, top, limit, slope):
    ranking = jax.random.permutation(stream_key, count)
    crowded, ordinary = portions_of(count, rows * top, limit, slope, True), portions_of(count, rows * top, limit, slope, False)
    places = jnp.arange(count)

    def named(tallies, rotation):
        used = int((tallies > 0).sum())
        fixed = max(1, used // 4)
        passed = fixed + (places - fixed + rotation * (used - fixed)) % max(1, count - fixed)
        return jnp.zeros((count,), jnp.int32).at[ranking[jnp.where(places < fixed, places, passed)]].set(jnp.asarray(tallies, jnp.int32))

    tallies = jnp.where(number % 4 == 0, named(crowded, number // 4), named(ordinary, number - number // 4 - 1))
    mixed = jax.random.permutation(jax.random.fold_in(own, 3), count)
    giver, taker = mixed[0:count // 2 * 2:2], mixed[1:count // 2 * 2:2]
    slack = jnp.minimum(tallies[giver] - 1, limit - tallies[taker]) // 2
    slack = jnp.where((giver == ranking[0]) | (taker == ranking[0]) | (tallies[taker] == 0), 0, jnp.maximum(slack, 0))
    passed = jax.random.randint(jax.random.fold_in(own, 4), (count // 2,), 0, 1 << 20) % (slack + 1)
    tallies = tallies.at[giver].add(-passed).at[taker].add(passed)
    labels = jnp.searchsorted(jnp.cumsum(tallies), jnp.arange(rows * top), side="right").astype(jnp.int32)
    listing = labels.reshape(top, rows).T
    listing = listing[jax.random.permutation(jax.random.fold_in(own, 1), rows)]
    rotation = jax.random.randint(jax.random.fold_in(own, 2), (rows, 1), 0, top)
    return jnp.take_along_axis(listing, (jnp.arange(top)[None, :] + rotation) % top, axis=1)


def portions_of(amount, total, limit, slope, full):
    loads = [(1 << 20) // math.isqrt(rank ** slope) + 1 for rank in range(1, amount + 1)]
    largest = limit if full else min(limit, max(-(-total // amount), total * loads[0] // sum(loads)))
    least = 1 if total - largest >= amount - 1 else 0
    given, surplus = [largest] + [least] * (amount - 1), total - largest - least * (amount - 1)
    while surplus > 0:
        movable = [i for i in range(1, amount) if given[i] < largest] or [i for i in range(1, amount) if given[i] < limit]
        pool, remaining = sum([loads[i] for i in movable]), surplus
        for i in movable:
            extra = min(limit - given[i], max(1, remaining * loads[i] // pool), surplus)
            given[i] = given[i] + extra
            surplus = surplus - extra
    return np.array(given)


def gaussian(key, extent, width, most, pieces=(), held_as=jnp.bfloat16):
    array = jax.random.normal(key, extent, jnp.float32) * width
    if len(pieces) > 0:
        array = shard_levels(key, extent, pieces, -0.22, 0.18) * array
    return jnp.clip(array, min=-most, max=most).astype(held_as)


def setup_inputs(seed: int = 0) -> dict:
    streams_of = jax.random.split(jax.random.key(seed), 17)
    layer_input = gaussian(streams_of[0], (ROWS, SEQ, D), 1.0, 6.0, ((0, 16), (1, 2)))
    attention_gain = jnp.clip(1.0 + 0.18 * jax.random.normal(streams_of[1], (D,), jnp.float32), 0.1, 1.9)
    query_gain = jnp.clip(jnp.exp(jax.random.uniform(streams_of[2], (HD,), jnp.float32, math.log(0.5), math.log(2.0))), 0.5, 2.0)
    key_gain = jnp.clip(jnp.exp(jax.random.uniform(streams_of[3], (HD,), jnp.float32, math.log(0.5), math.log(2.0))), 0.5, 2.0)
    query_weight = gaussian(streams_of[4], (D, H * HD), D ** -0.5, 0.125, ((0, 16), (1, 2)))
    key_weight = gaussian(streams_of[5], (D, KVH * HD), D ** -0.5, 0.125, ((0, 16), (1, 2)))
    value_weight = gaussian(streams_of[6], (D, KVH * HD), D ** -0.5, 0.125, ((0, 16), (1, 2)))
    output_weight = gaussian(streams_of[7], (D, H * HD), (H * HD // 32) ** -0.5, 0.5, ((0, 16), (1, 2)))
    router_weight = gaussian(streams_of[8], (D, EXPERTS), D ** -0.5, 0.125, ((0, 16),))
    expert_gain = jnp.clip(1.0 + 0.18 * jax.random.normal(streams_of[9], (D,), jnp.float32), 0.1, 1.9)
    gate_weight = gaussian(streams_of[10], (EXPERTS, D, FFE), D ** -0.5, 0.125, ((0, 16), (2, 2)))
    up_weight = gaussian(streams_of[11], (EXPERTS, D, FFE), D ** -0.5, 0.125, ((0, 16), (2, 2)))
    down_weight = gaussian(streams_of[12], (EXPERTS, FFE, D), (FFE // 8) ** -0.5, 0.625, ((0, 16), (1, 2)))
    routes_keys = jax.random.split(jax.random.fold_in(streams_of[13], 1), ROWS * SEQ // (ROWS_DEV * SEQ))
    routes_turns = jax.random.permutation(jax.random.fold_in(streams_of[13], 3), ROWS * SEQ // (ROWS_DEV * SEQ))
    routes = jax.vmap(lambda own, number: routed_block(jax.random.fold_in(streams_of[13], 2), own, number, ROWS_DEV * SEQ, EXPERTS, TOPK, CAP, 1))(routes_keys, routes_turns).reshape((ROWS, SEQ, TOPK))
    segments = jax.vmap(lambda own: jnp.searchsorted(jnp.cumsum(ragged(own, 4, SEQ, SEQ // 2, 1)), jnp.arange(SEQ), side="right"))(jax.random.split(streams_of[14], ROWS)).reshape((ROWS, SEQ)).astype(jnp.int32)
    cotangent = gaussian(streams_of[15], (ROWS, SEQ, D), 1.0, 6.0, ((0, 16), (1, 2)))
    return {"layer_input": layer_input, "attention_gain": attention_gain, "query_gain": query_gain, "key_gain": key_gain, "query_weight": query_weight, "key_weight": key_weight, "value_weight": value_weight, "output_weight": output_weight, "router_weight": router_weight, "expert_gain": expert_gain, "gate_weight": gate_weight, "up_weight": up_weight, "down_weight": down_weight, "routes": routes, "segments": segments, "cotangent": cotangent}


EPSILON = 1e-06
ROPE_BASE = 1000000.0
NEGATIVE = -1e+30

def inverse_rms(values):
    return lax.rsqrt(lax.optimization_barrier(jnp.mean(values * values, axis=-1, keepdims=True)) + EPSILON)

def norm_backward(grad_scaled, gain, normed, inverse):
    grad_normed = grad_scaled * gain
    return inverse * (grad_normed - normed * lax.optimization_barrier(jnp.mean(grad_normed * normed, axis=-1, keepdims=True)))

def rotary_tables(segment_ids, head_size):
    length = segment_ids.shape[1]
    starts = lax.optimization_barrier(jnp.sum((segment_ids[:, None, :] < segment_ids[:, :, None]).astype(jnp.int32), axis=2)).astype(jnp.int32)
    places = jnp.arange(length, dtype=jnp.int32)[None, :] - starts
    half_size = head_size // 2
    frequency = jnp.exp(jnp.arange(half_size, dtype=jnp.float32) * (-2.0 * math.log(ROPE_BASE) / head_size))
    angles = places.astype(jnp.float32)[:, :, None] * frequency
    return (jnp.cos(angles), jnp.sin(angles))

def rotate(values, cosine_table, sine_table):
    half_size = values.shape[-1] // 2
    front_half = values[..., :half_size]
    back_half = values[..., half_size:]
    cosine = cosine_table[:, :, None, :]
    sine_part = sine_table[:, :, None, :]
    return jnp.concatenate([front_half * cosine - back_half * sine_part, back_half * cosine + front_half * sine_part], axis=-1)

def unrotate(grads, cosine_table, sine_table):
    half_size = grads.shape[-1] // 2
    front_half = grads[..., :half_size]
    back_half = grads[..., half_size:]
    cosine = cosine_table[:, :, None, :]
    sine_part = sine_table[:, :, None, :]
    return jnp.concatenate([front_half * cosine + back_half * sine_part, back_half * cosine - front_half * sine_part], axis=-1)

def segment_mask(segment_ids):
    length = segment_ids.shape[1]
    places = jnp.arange(length, dtype=jnp.int32)
    causal = places[None, :] <= places[:, None]
    return (segment_ids[:, :, None] == segment_ids[:, None, :]) & causal[None]

def attend_row(operands):
    query_rot, key_rot, value_rows, allowed = operands
    factor = 1.0 / math.sqrt(query_rot.shape[-1])
    scores = jnp.einsum('ingc,jnc->ngij', query_rot.astype(jnp.float32), key_rot.astype(jnp.float32)) * factor
    scores = jnp.where(allowed[None, None], scores, NEGATIVE)
    row_max = lax.optimization_barrier(jnp.max(scores, axis=-1, keepdims=True))
    log_total = row_max + jnp.log(lax.optimization_barrier(jnp.sum(jnp.exp(scores - row_max), axis=-1, keepdims=True)))
    attention_weights = jnp.exp(scores - log_total).astype(jnp.bfloat16)
    attended = jnp.einsum('ngij,jnc->ingc', attention_weights.astype(jnp.float32), value_rows.astype(jnp.float32)).astype(jnp.bfloat16)
    return (attended, log_total[..., 0])

def attend_back(operands):
    query_rot, key_rot, value_rows, allowed, log_total, attended, grad_out = operands
    factor = 1.0 / math.sqrt(query_rot.shape[-1])
    scores = jnp.einsum('ingc,jnc->ngij', query_rot.astype(jnp.float32), key_rot.astype(jnp.float32)) * factor
    scores = jnp.where(allowed[None, None], scores, NEGATIVE)
    attention_weights = jnp.exp(scores - log_total[..., None])
    grad_wide = grad_out.astype(jnp.float32)
    grad_value = jnp.einsum('ngij,ingc->jnc', attention_weights.astype(jnp.bfloat16).astype(jnp.float32), grad_wide)
    grad_weights = jnp.einsum('ingc,jnc->ngij', grad_wide, value_rows.astype(jnp.float32))
    row_delta = jnp.einsum('ingc,ingc->ngi', attended.astype(jnp.float32), grad_wide)
    grad_scores = (attention_weights * (grad_weights - row_delta[..., None]) * factor).astype(jnp.bfloat16).astype(jnp.float32)
    grad_query = jnp.einsum('ngij,jnc->ingc', grad_scores, key_rot.astype(jnp.float32))
    grad_key = jnp.einsum('ngij,ingc->jnc', grad_scores, query_rot.astype(jnp.float32))
    return (grad_query, grad_key, grad_value)

def attention_forward(group_input, group_segments, attention_gain, query_gain, key_gain, query_weight, key_weight, value_weight, output_weight):
    row_count, length, model_width = group_input.shape
    token_count = row_count * length
    head_size = query_gain.shape[0]
    kv_count = key_weight.shape[1] // head_size
    group_size = query_weight.shape[1] // key_weight.shape[1]
    input_wide = group_input.astype(jnp.float32).reshape(token_count, model_width)
    inverse_one = inverse_rms(input_wide)
    normed_one = input_wide * inverse_one
    attention_rows = (normed_one * attention_gain).astype(jnp.bfloat16)
    query_pre = jnp.dot(attention_rows, query_weight, preferred_element_type=jnp.float32).reshape(row_count, length, kv_count * group_size, head_size)
    key_pre = jnp.dot(attention_rows, key_weight, preferred_element_type=jnp.float32).reshape(row_count, length, kv_count, head_size)
    value_rows = jnp.dot(attention_rows, value_weight, preferred_element_type=jnp.float32).astype(jnp.bfloat16).reshape(row_count, length, kv_count, head_size)
    cosine_table, sine_table = rotary_tables(group_segments, head_size)
    inverse_query = inverse_rms(query_pre)
    normed_query = query_pre * inverse_query
    inverse_key = inverse_rms(key_pre)
    normed_key = key_pre * inverse_key
    query_rot = rotate(normed_query * query_gain, cosine_table, sine_table).astype(jnp.bfloat16).reshape(row_count, length, kv_count, group_size, head_size)
    key_rot = rotate(normed_key * key_gain, cosine_table, sine_table).astype(jnp.bfloat16)
    allowed = segment_mask(group_segments)
    attended, log_total = lax.map(attend_row, (query_rot, key_rot, value_rows, allowed))
    attended_flat = attended.reshape(token_count, kv_count * group_size * head_size)
    middle = input_wide + jnp.dot(attended_flat, output_weight.T, preferred_element_type=jnp.float32)
    return (middle, attention_rows, inverse_one, normed_one, normed_query, inverse_query, normed_key, inverse_key, query_rot, key_rot, value_rows, attended, log_total, cosine_table, sine_table, allowed)

def reference(layer_input, attention_gain, query_gain, key_gain, query_weight, key_weight, value_weight, output_weight, router_weight, expert_gain, gate_weight, up_weight, down_weight, routes, segments, cotangent):
    model_width = D
    tokens = ROWS * SEQ
    group_count = N_FSDP
    assigned = tokens * TOPK
    per_group = ROWS_DEV * SEQ * TOPK
    half_hidden = FFE // N_TP
    input_groups = layer_input.reshape(group_count, ROWS_DEV, SEQ, model_width)
    segment_groups = segments.reshape(group_count, ROWS_DEV, SEQ)

    def forward_group(operands):
        group_input, group_segments = operands
        return attention_forward(group_input, group_segments, attention_gain, query_gain, key_gain, query_weight, key_weight, value_weight, output_weight)[0]
    middle = lax.map(forward_group, (input_groups, segment_groups)).reshape(tokens, model_width)
    inverse_two = inverse_rms(middle)
    normed_two = middle * inverse_two
    expert_rows = (normed_two * expert_gain).astype(jnp.bfloat16)
    logits = jnp.dot(expert_rows, router_weight, preferred_element_type=jnp.float32)
    route_flat = routes.reshape(tokens, TOPK)
    chosen_mask = route_flat[:, :, None] == jnp.arange(EXPERTS, dtype=jnp.int32)
    chosen = lax.optimization_barrier(jnp.sum(jnp.where(chosen_mask, logits[:, None, :], 0.0), axis=-1))
    gate_probs = jax.nn.softmax(chosen, axis=-1)
    route_groups = routes.reshape(group_count, per_group)
    member = (route_groups[:, :, None] == jnp.arange(EXPERTS, dtype=jnp.int32)).astype(jnp.int32)
    slot_index = lax.optimization_barrier(jnp.sum((jnp.cumsum(member, axis=1) - member) * member, axis=2)).astype(jnp.int32)
    place_index = (route_groups * (group_count * CAP) + jnp.arange(group_count, dtype=jnp.int32)[:, None] * CAP + slot_index).astype(jnp.int32)
    owner_index = jnp.full((EXPERTS * group_count * CAP,), assigned, jnp.int32).at[place_index.reshape(assigned)].set(jnp.arange(assigned, dtype=jnp.int32))
    owner_index = owner_index.reshape(EXPERTS, group_count * CAP)
    padded_rows = jnp.concatenate([expert_rows, jnp.zeros((1, model_width), jnp.bfloat16)], axis=0)
    cot_flat = cotangent.reshape(tokens, model_width)
    padded_cot = jnp.concatenate([cot_flat, jnp.zeros((1, model_width), jnp.bfloat16)], axis=0)
    padded_gates = jnp.concatenate([gate_probs.reshape(assigned), jnp.zeros((1,), jnp.float32)], axis=0)

    def expert_step(carry, operands):
        moe_total, grad_total, grad_gate = carry
        owned, gate_mat, up_mat, down_mat = operands
        token_index = owned // TOPK
        place_rows = padded_rows[token_index]
        place_gates = padded_gates[owned]
        cot_wide = padded_cot[token_index].astype(jnp.float32)
        scaled = (place_gates[:, None] * cot_wide).astype(jnp.bfloat16)
        gate_parts = []
        up_parts = []
        down_parts = []
        for half_index in range(N_TP):
            low = half_index * half_hidden
            gate_half = gate_mat[:, low:low + half_hidden]
            up_half = up_mat[:, low:low + half_hidden]
            down_half = down_mat[low:low + half_hidden, :]
            gate_pre = jnp.dot(place_rows, gate_half, preferred_element_type=jnp.float32)
            up_pre = jnp.dot(place_rows, up_half, preferred_element_type=jnp.float32)
            activated = jax.nn.silu(gate_pre)
            hidden = (activated * up_pre).astype(jnp.bfloat16)
            expert_out = jnp.dot(hidden, down_half, preferred_element_type=jnp.float32).astype(jnp.bfloat16)
            out_wide = expert_out.astype(jnp.float32)
            moe_total = moe_total.at[token_index].add(place_gates[:, None] * out_wide)
            grad_gate = grad_gate.at[half_index, owned].add(lax.optimization_barrier(jnp.sum(cot_wide * out_wide, axis=1)))
            grad_hidden = jnp.dot(scaled, down_half.T, preferred_element_type=jnp.float32)
            sigmoid_gate = jax.nn.sigmoid(gate_pre)
            grad_gate_pre = (grad_hidden * up_pre * sigmoid_gate * (1.0 + gate_pre * (1.0 - sigmoid_gate))).astype(jnp.bfloat16)
            grad_up_pre = (grad_hidden * activated).astype(jnp.bfloat16)
            down_parts.append(jnp.dot(hidden.T, scaled, preferred_element_type=jnp.float32))
            gate_parts.append(jnp.dot(place_rows.T, grad_gate_pre, preferred_element_type=jnp.float32))
            up_parts.append(jnp.dot(place_rows.T, grad_up_pre, preferred_element_type=jnp.float32))
            grad_places = (jnp.dot(grad_gate_pre, gate_half.T, preferred_element_type=jnp.float32) + jnp.dot(grad_up_pre, up_half.T, preferred_element_type=jnp.float32)).astype(jnp.bfloat16)
            grad_total = grad_total.at[token_index].add(grad_places.astype(jnp.float32))
        return ((moe_total, grad_total, grad_gate), (jnp.concatenate(gate_parts, axis=1), jnp.concatenate(up_parts, axis=1), jnp.concatenate(down_parts, axis=0)))
    start = (jnp.zeros((tokens + 1, model_width), jnp.float32), jnp.zeros((tokens + 1, model_width), jnp.float32), jnp.zeros((N_TP, assigned + 1), jnp.float32))
    (moe_total, grad_total, grad_gate), (gate_grad, up_grad, down_grad) = lax.scan(expert_step, start, (owner_index, gate_weight, up_weight, down_weight))
    layer_output = (middle + moe_total[:tokens]).astype(jnp.bfloat16).reshape(ROWS, SEQ, model_width)
    grad_expert = grad_total[:tokens]
    router_grad = jnp.zeros((model_width, EXPERTS), jnp.float32)
    for half_index in range(N_TP):
        part = grad_gate[half_index, :assigned].reshape(tokens, TOPK)
        grad_chosen = gate_probs * (part - lax.optimization_barrier(jnp.sum(gate_probs * part, axis=-1, keepdims=True)))
        grad_logits = lax.optimization_barrier(jnp.sum(jnp.where(chosen_mask, grad_chosen[:, :, None], 0.0), axis=1)).astype(jnp.bfloat16)
        router_grad = router_grad + jnp.dot(expert_rows.T, grad_logits, preferred_element_type=jnp.float32)
        grad_expert = grad_expert + jnp.dot(grad_logits, router_weight.T, preferred_element_type=jnp.float32)
    expert_gain_grad = lax.optimization_barrier(jnp.sum(grad_expert * normed_two, axis=0))
    grad_middle = cot_flat.astype(jnp.float32) + norm_backward(grad_expert, expert_gain, normed_two, inverse_two)
    grad_groups = grad_middle.reshape(group_count, ROWS_DEV * SEQ, model_width)

    def backward_group(carry, operands):
        acc_query, acc_key, acc_value, acc_output, acc_qgain, acc_kgain, acc_again = carry
        group_input, group_segments, grad_mid = operands
        group_middle, attention_rows, inverse_one, normed_one, normed_query, inverse_query, normed_key, inverse_key, query_rot, key_rot, value_rows, attended, log_total, cosine_table, sine_table, allowed = attention_forward(group_input, group_segments, attention_gain, query_gain, key_gain, query_weight, key_weight, value_weight, output_weight)
        row_count, length, kv_count, group_size, head_size = query_rot.shape
        token_count = row_count * length
        grad_low = grad_mid.astype(jnp.bfloat16)
        attended_flat = attended.reshape(token_count, kv_count * group_size * head_size)
        grad_attended = jnp.dot(grad_low, output_weight, preferred_element_type=jnp.float32).astype(jnp.bfloat16).reshape(row_count, length, kv_count, group_size, head_size)
        output_part = jnp.dot(grad_low.T, attended_flat, preferred_element_type=jnp.float32)
        grad_query_rot, grad_key_rot, grad_value = lax.map(attend_back, (query_rot, key_rot, value_rows, allowed, log_total, attended, grad_attended))
        grad_query_norm = unrotate(grad_query_rot.reshape(row_count, length, kv_count * group_size, head_size), cosine_table, sine_table)
        grad_key_norm = unrotate(grad_key_rot, cosine_table, sine_table)
        qgain_part = lax.optimization_barrier(jnp.sum(grad_query_norm * normed_query, axis=(0, 1, 2)))
        kgain_part = lax.optimization_barrier(jnp.sum(grad_key_norm * normed_key, axis=(0, 1, 2)))
        grad_query_pre = norm_backward(grad_query_norm, query_gain, normed_query, inverse_query).reshape(token_count, -1).astype(jnp.bfloat16)
        grad_key_pre = norm_backward(grad_key_norm, key_gain, normed_key, inverse_key).reshape(token_count, -1).astype(jnp.bfloat16)
        grad_value_low = grad_value.reshape(token_count, -1).astype(jnp.bfloat16)
        query_part = jnp.dot(attention_rows.T, grad_query_pre, preferred_element_type=jnp.float32)
        key_part = jnp.dot(attention_rows.T, grad_key_pre, preferred_element_type=jnp.float32)
        value_part = jnp.dot(attention_rows.T, grad_value_low, preferred_element_type=jnp.float32)
        grad_one = jnp.dot(grad_query_pre, query_weight.T, preferred_element_type=jnp.float32) + jnp.dot(grad_key_pre, key_weight.T, preferred_element_type=jnp.float32) + jnp.dot(grad_value_low, value_weight.T, preferred_element_type=jnp.float32)
        again_part = lax.optimization_barrier(jnp.sum(grad_one * normed_one, axis=0))
        grad_in = grad_mid + norm_backward(grad_one, attention_gain, normed_one, inverse_one)
        new_carry = (acc_query + query_part.astype(jnp.bfloat16).astype(jnp.float32), acc_key + key_part.astype(jnp.bfloat16).astype(jnp.float32), acc_value + value_part.astype(jnp.bfloat16).astype(jnp.float32), acc_output + output_part.astype(jnp.bfloat16).astype(jnp.float32), acc_qgain + qgain_part, acc_kgain + kgain_part, acc_again + again_part)
        return (new_carry, grad_in)
    zero_carry = (jnp.zeros((model_width, H * HD), jnp.float32), jnp.zeros((model_width, KVH * HD), jnp.float32), jnp.zeros((model_width, KVH * HD), jnp.float32), jnp.zeros((model_width, H * HD), jnp.float32), jnp.zeros((HD,), jnp.float32), jnp.zeros((HD,), jnp.float32), jnp.zeros((model_width,), jnp.float32))
    (query_grad, key_grad, value_grad, output_grad, query_gain_grad, key_gain_grad, attention_gain_grad), input_grad = lax.scan(backward_group, zero_carry, (input_groups, segment_groups, grad_groups))
    input_grad = input_grad.reshape(ROWS, SEQ, model_width)
    return (layer_output, input_grad, attention_gain_grad, query_gain_grad, key_gain_grad, query_grad, key_grad, value_grad, output_grad, router_grad, expert_gain_grad, gate_grad, up_grad, down_grad)
```

```python
import functools
import math

import jax
import jax.numpy as jnp
from jax import lax
from jax.experimental import pallas as pl
from jax.experimental.pallas import tpu as pltpu
from jax.sharding import PartitionSpec as P

EPSILON = 1e-06
ROPE_BASE = 1000000.0
NEGATIVE = -1e30
F32 = jnp.float32
BF16 = jnp.bfloat16


def inverse_rms(values):
    return lax.rsqrt(jnp.mean(values * values, axis=-1, keepdims=True) + EPSILON)


def norm_backward(grad_scaled, gain, normed, inverse):
    grad_normed = grad_scaled * gain
    return inverse * (grad_normed - normed * jnp.mean(grad_normed * normed, axis=-1, keepdims=True))


def mm(a, b, dims=((1,), (0,))):
    return lax.dot_general(a, b, (dims, ((), ())), preferred_element_type=F32)


def fetch_next(values, step):
    size = lax.axis_size("tp")
    return lax.ppermute(values, "tp", [(s, (s - step) % size) for s in range(size)])


def gather_tp(values, axis):
    size = lax.axis_size("tp")
    return jnp.concatenate([values] + [fetch_next(values, j) for j in range(1, size)], axis=axis)


def scatter_tp(pieces):
    size = lax.axis_size("tp")
    total = pieces[0].astype(F32)
    for j in range(1, size):
        moved = lax.ppermute(
            pieces[j].astype(BF16), "tp", [(s, (s + j) % size) for s in range(size)]
        )
        total = total + moved.astype(F32)
    return total


def turn(values, cosine, sine):
    return values * cosine + pltpu.roll(values, values.shape[-1] // 2, 1) * sine


def turn_back(values, cosine, sine):
    return values * cosine - pltpu.roll(values, values.shape[-1] // 2, 1) * sine


def normed_turned(pre, gain, cosine, sine):
    inverse = inverse_rms(pre)
    normed = pre * inverse
    return inverse, normed, turn(normed * gain, cosine, sine).astype(BF16)


def weights_of(query_rot, key_rot, bias):
    factor = 1.0 / math.sqrt(query_rot.shape[-1])
    scores = mm(query_rot, key_rot, ((1,), (1,))) * factor + bias
    powers = jnp.exp(scores - jnp.max(scores, axis=-1, keepdims=True))
    return powers * (1.0 / jnp.sum(powers, axis=-1, keepdims=True))


def attend_kernel(q_ref, k_ref, v_ref, cos_ref, sin_ref, bias_ref, qg_ref, kg_ref, out_ref, key_rot):
    cosine, sine = cos_ref[...], sin_ref[...]

    @pl.when(pl.program_id(2) == 0)
    def _():
        key_rot[...] = normed_turned(k_ref[...], kg_ref[...], cosine, sine)[2]

    query_rot = normed_turned(q_ref[...], qg_ref[...], cosine, sine)[2]
    weights = weights_of(query_rot, key_rot[...], bias_ref[...])
    out_ref[...] = mm(weights.astype(BF16), v_ref[...].astype(BF16)).astype(BF16)


def attend_back_kernel(
    q_ref, k_ref, v_ref, cos_ref, sin_ref, bias_ref, qg_ref, kg_ref, att_ref, go_ref,
    grad_ref, qgain_ref, kgain_ref, key_rot, key_normed, key_inverse, grad_key, grad_value,
):
    row, kv, step = pl.program_id(0), pl.program_id(1), pl.program_id(2)
    group_size = pl.num_programs(2) - 2
    cosine, sine = cos_ref[...], sin_ref[...]
    factor = 1.0 / math.sqrt(q_ref.shape[-1])

    @pl.when((row == 0) & (kv == 0) & (step == 0))
    def _():
        qgain_ref[...] = jnp.zeros_like(qgain_ref)
        kgain_ref[...] = jnp.zeros_like(kgain_ref)

    @pl.when(step == 0)
    def _():
        inverse, normed, rotated = normed_turned(k_ref[...], kg_ref[...], cosine, sine)
        key_rot[...] = rotated
        key_normed[...] = normed
        key_inverse[...] = jnp.broadcast_to(inverse, key_inverse.shape)
        grad_key[...] = jnp.zeros_like(grad_key)
        grad_value[...] = jnp.zeros_like(grad_value)

    @pl.when(step < group_size)
    def _():
        inverse, normed, query_rot = normed_turned(q_ref[...], qg_ref[...], cosine, sine)
        weights = weights_of(query_rot, key_rot[...], bias_ref[...])
        grad_out = go_ref[...]
        grad_value[...] += mm(weights.astype(BF16), grad_out, ((0,), (0,)))
        grad_weights = mm(grad_out, v_ref[...].astype(BF16), ((1,), (1,)))
        delta = jnp.sum(att_ref[...].astype(F32) * grad_out.astype(F32), axis=-1, keepdims=True)
        grad_scores = (weights * (grad_weights - delta) * factor).astype(BF16)
        grad_query = turn_back(mm(grad_scores, key_rot[...]), cosine, sine)
        grad_key[...] += mm(grad_scores, query_rot, ((0,), (0,)))
        qgain_ref[...] += jnp.sum(grad_query * normed, axis=0, keepdims=True)
        grad_ref[...] = norm_backward(grad_query, qg_ref[...], normed, inverse).astype(BF16)

    @pl.when(step == group_size)
    def _():
        grad = turn_back(grad_key[...], cosine, sine)
        normed = key_normed[...]
        kgain_ref[...] += jnp.sum(grad * normed, axis=0, keepdims=True)
        grad_ref[...] = norm_backward(
            grad, kg_ref[...], normed, key_inverse[...][:, :1]
        ).astype(BF16)

    @pl.when(step == group_size + 1)
    def _():
        grad_ref[...] = grad_value[...].astype(BF16)


def attention_specs(length, head_size, heads, kv_heads):
    group_size = heads // kv_heads

    def head(r, kv, g):
        return (r, kv * group_size + jnp.minimum(g, group_size - 1))

    block = (length, head_size)
    full = pl.BlockSpec((1, head_size), lambda r, kv, g: (0, 0))
    return head, [
        pl.BlockSpec(block, head),
        pl.BlockSpec(block, lambda r, kv, g: (r, heads + kv)),
        pl.BlockSpec(block, lambda r, kv, g: (r, heads + kv_heads + kv)),
        pl.BlockSpec(block, lambda r, kv, g: (r, 0)),
        pl.BlockSpec(block, lambda r, kv, g: (r, 0)),
        pl.BlockSpec((None, length, length), lambda r, kv, g: (r, 0, 0)),
        full,
        full,
    ]


def attend(pre, tables, gains, rows, heads, kv_heads):
    length, head_size = pre.shape[0] // rows, gains[0].shape[1]
    head, specs = attention_specs(length, head_size, heads, kv_heads)
    cost = rows * heads * length * length
    return pl.pallas_call(
        attend_kernel,
        grid=(rows, kv_heads, heads // kv_heads),
        in_specs=specs,
        out_specs=pl.BlockSpec((length, head_size), head),
        out_shape=jax.ShapeDtypeStruct((pre.shape[0], heads * head_size), BF16),
        scratch_shapes=[pltpu.VMEM((length, head_size), BF16)],
        cost_estimate=pl.CostEstimate(
            flops=4 * cost * head_size, bytes_accessed=6 * pre.size, transcendentals=cost
        ),
        name="attend",
    )(pre, pre, pre, *tables, *gains)


def attend_back(pre, tables, gains, attended, grad_attended, rows, heads, kv_heads):
    length, head_size = pre.shape[0] // rows, gains[0].shape[1]
    group_size = heads // kv_heads
    head, specs = attention_specs(length, head_size, heads, kv_heads)

    def target(r, kv, g):
        own = kv * group_size + g
        return (r, jnp.where(g < group_size, own, heads + kv + jnp.where(g > group_size, kv_heads, 0)))

    block = pl.BlockSpec((length, head_size), head)
    full = pl.BlockSpec((1, head_size), lambda r, kv, g: (0, 0))
    gain = jax.ShapeDtypeStruct((1, head_size), F32)
    cost = rows * heads * length * length
    wide = pltpu.VMEM((length, head_size), F32)
    return pl.pallas_call(
        attend_back_kernel,
        grid=(rows, kv_heads, group_size + 2),
        in_specs=specs + [block, block],
        out_specs=[pl.BlockSpec((length, head_size), target), full, full],
        out_shape=[jax.ShapeDtypeStruct(pre.shape, BF16), gain, gain],
        scratch_shapes=[pltpu.VMEM((length, head_size), BF16), wide, wide, wide, wide],
        cost_estimate=pl.CostEstimate(
            flops=10 * cost * head_size, bytes_accessed=10 * pre.size, transcendentals=cost
        ),
        name="attend_back",
    )(pre, pre, pre, *tables, *gains, attended, grad_attended)


def local(
    layer_input,
    attention_gain,
    query_gain,
    key_gain,
    query_weight,
    key_weight,
    value_weight,
    output_weight,
    router_weight,
    expert_gain,
    gate_weight,
    up_weight,
    down_weight,
    routes,
    segments,
    cotangent,
):
    rows, local_length, model_width = layer_input.shape
    length = segments.shape[1]
    head_size = query_gain.shape[0]
    expert_count = router_weight.shape[1]
    local_experts, _, half_hidden = gate_weight.shape
    top_count = routes.shape[2]
    nodes = lax.axis_size("fsdp")
    tp_size = lax.axis_size("tp")
    node = lax.axis_index("fsdp")
    part = lax.axis_index("tp")
    heads = query_weight.shape[1] // head_size
    kv_heads = key_weight.shape[1] // head_size
    hidden_size = half_hidden * tp_size
    capacity = max(2, rows * length * top_count * 5 // (4 * expert_count))
    tokens = rows * local_length
    places = min(capacity, tokens)
    every = tp_size * tokens

    qkv_full = lax.all_gather(
        jnp.concatenate([query_weight, key_weight, value_weight], axis=1), "fsdp", axis=0, tiled=True
    )
    input_wide = layer_input.astype(F32)
    inverse_one = inverse_rms(input_wide)
    normed_one = input_wide * inverse_one
    normed_low = (normed_one * attention_gain).astype(BF16)
    normed_rows = gather_tp(normed_low, 1).reshape(every, model_width)
    output_full = lax.all_gather(output_weight, "fsdp", axis=0, tiled=True)
    router_full = lax.all_gather(router_weight, "fsdp", axis=0, tiled=True)

    places_in = jnp.concatenate(
        [
            ((part + j) % tp_size) * local_length + jnp.arange(local_length, dtype=jnp.int32)
            for j in range(tp_size)
        ]
    )
    doubled = jnp.concatenate([segments, segments], axis=1)
    ids = lax.dynamic_slice_in_dim(doubled, part * local_length, length, axis=1)
    starts = jnp.sum((segments[:, None, :] < ids[:, :, None]).astype(jnp.int32), axis=2)
    half_size = head_size // 2
    frequency = jnp.exp(jnp.arange(half_size, dtype=F32) * (-2.0 * math.log(ROPE_BASE) / head_size))
    angles = (places_in[None, :] - starts).astype(F32)[:, :, None] * frequency
    cosine, sine = jnp.cos(angles), jnp.sin(angles)
    cosine_table = jnp.concatenate([cosine, cosine], axis=-1).reshape(every, head_size)
    sine_table = jnp.concatenate([-sine, sine], axis=-1).reshape(every, head_size)
    allowed = (ids[:, :, None] == ids[:, None, :]) & (places_in[None, :] <= places_in[:, None])[None]
    tables = (cosine_table, sine_table, jnp.where(allowed, 0.0, NEGATIVE).astype(F32))
    gains = (query_gain.reshape(1, head_size), key_gain.reshape(1, head_size))

    gate_weight, up_weight, down_weight, normed_rows = lax.optimization_barrier(
        (gate_weight, up_weight, down_weight, normed_rows)
    )
    gate_full = gather_tp(gate_weight, 2)
    up_full = gather_tp(up_weight, 2)
    down_full = gather_tp(down_weight, 1)

    own_routes = lax.dynamic_slice_in_dim(routes, part * local_length, local_length, axis=1)
    own_routes = own_routes.reshape(tokens, top_count)
    all_routes = lax.all_gather(own_routes, "fsdp", axis=0).reshape(nodes, tokens, top_count)
    own_experts = node * local_experts + jnp.arange(local_experts, dtype=jnp.int32)
    member = jnp.any(all_routes[:, None, :, :] == own_experts[None, :, None, None], axis=-1)
    before = jnp.arange(tokens)[:, None] < jnp.arange(tokens)[None, :]
    slot = jnp.einsum(
        "get,tu->geu", member.astype(BF16), before.astype(BF16), preferred_element_type=F32
    ).astype(jnp.int32)
    slot = jnp.where(member, slot, -1)
    placed = slot[:, :, None, :] == jnp.arange(places, dtype=jnp.int32)[None, None, :, None]

    pre = mm(normed_rows, qkv_full)
    attended = attend(pre, tables, gains, rows, heads, kv_heads)
    projected = mm(attended, output_full, ((1,), (1,))).reshape(rows, tp_size, local_length, model_width)
    middle = input_wide + scatter_tp([projected[:, j] for j in range(tp_size)])
    inverse_two = inverse_rms(middle)
    normed_two = middle * inverse_two
    expert_low = (normed_two * expert_gain).astype(BF16).reshape(tokens, model_width)

    rows_all = lax.all_gather(expert_low, "fsdp", axis=0)
    logits = mm(expert_low, router_full)
    chosen = jnp.any(
        own_routes[:, :, None] == jnp.arange(expert_count, dtype=jnp.int32), axis=1
    )
    top = jnp.max(jnp.where(chosen, logits, NEGATIVE), axis=-1, keepdims=True)
    powers = jnp.where(chosen, jnp.exp(jnp.minimum(logits - top, 0.0)), 0.0)
    gates = powers / jnp.sum(powers, axis=-1, keepdims=True)
    gates_all = lax.all_gather(gates, "fsdp", axis=0)
    cot_low = cotangent.reshape(tokens, model_width)
    cot_all = lax.all_gather(cot_low, "fsdp", axis=0)
    own_gates = lax.dynamic_slice_in_dim(gates_all, node * local_experts, local_experts, axis=2)
    gate_of = jnp.sum(
        jnp.where(placed, jnp.moveaxis(own_gates, 2, 1)[:, :, None, :], 0.0), axis=-1
    )

    out_total = None
    grad_total = None
    gate_columns = []
    own_grads = []
    far_grads = []
    for e in range(local_experts):
        spread = placed[:, e].astype(BF16)
        gate_here = gate_of[:, e].reshape(nodes * places, 1)
        arrived = jnp.einsum("gst,gtd->gsd", spread, rows_all, preferred_element_type=F32)
        arrived = arrived.astype(BF16).reshape(nodes * places, model_width)
        gate_pre = mm(arrived, gate_full[e])
        up_pre = mm(arrived, up_full[e])
        cots = jnp.einsum("gst,gtd->gsd", spread, cot_all, preferred_element_type=F32)
        cots = cots.astype(BF16).reshape(nodes * places, model_width)
        grad_plain = mm(cots, down_full[e], ((1,), (1,)))
        sigmoid_gate = jax.nn.sigmoid(gate_pre)
        activated = gate_pre * sigmoid_gate
        hidden = activated * up_pre
        gate_columns.append(jnp.sum(hidden * grad_plain, axis=-1).reshape(nodes, places))
        grad_hidden = grad_plain * gate_here
        grad_gate_pre = (
            grad_hidden * up_pre * sigmoid_gate * (1.0 + gate_pre * (1.0 - sigmoid_gate))
        ).astype(BF16)
        grad_up_pre = (grad_hidden * activated).astype(BF16)
        weighed = (hidden * gate_here).astype(BF16)
        grad_places = (
            mm(grad_gate_pre, gate_full[e], ((1,), (1,))) + mm(grad_up_pre, up_full[e], ((1,), (1,)))
        ).astype(BF16).reshape(nodes, places, model_width)
        produced = mm(weighed, down_full[e]).astype(BF16).reshape(nodes, places, model_width)
        out_here = jnp.einsum("gst,gsd->gtd", spread, produced, preferred_element_type=F32)
        grad_here = jnp.einsum("gst,gsd->gtd", spread, grad_places, preferred_element_type=F32)
        if out_total is not None:
            out_here = out_here + out_total.astype(F32)
            grad_here = grad_here + grad_total.astype(F32)
        out_total = out_here.astype(BF16)
        grad_total = grad_here.astype(BF16)
        grads = (
            mm(arrived, grad_gate_pre, ((0,), (0,))),
            mm(arrived, grad_up_pre, ((0,), (0,))),
            mm(weighed, cots, ((0,), (0,))),
        )
        own_grads.append(
            (grads[0][:, :half_hidden], grads[1][:, :half_hidden], grads[2][:half_hidden])
        )
        far_grads.append(
            [
                (
                    grads[0][:, j * half_hidden : (j + 1) * half_hidden].astype(BF16),
                    grads[1][:, j * half_hidden : (j + 1) * half_hidden].astype(BF16),
                    grads[2][j * half_hidden : (j + 1) * half_hidden].astype(BF16),
                )
                for j in range(1, tp_size)
            ]
        )

    column = jnp.sum(
        jnp.where(placed, jnp.stack(gate_columns, axis=1)[:, :, :, None], 0.0), axis=2
    )
    column = jnp.moveaxis(column, 1, 2)
    grad_gate = lax.all_to_all(column, "fsdp", split_axis=0, concat_axis=0, tiled=True)
    grad_gate = jnp.moveaxis(grad_gate, 0, 1).reshape(tokens, expert_count)

    grad_rows = lax.psum_scatter(grad_total, "fsdp", scatter_dimension=0, tiled=True)
    expert_part = lax.psum_scatter(out_total, "fsdp", scatter_dimension=0, tiled=True)
    layer_output = (middle + expert_part.reshape(middle.shape).astype(F32)).astype(BF16)

    grad_logits = (
        gates * (grad_gate - jnp.sum(gates * grad_gate, axis=-1, keepdims=True))
    ).astype(BF16)
    router_part = mm(expert_low, grad_logits, ((0,), (0,)))
    grad_two = grad_rows.reshape(tokens, model_width).astype(F32) + mm(
        grad_logits, router_full, ((1,), (1,))
    )
    grad_two = grad_two.reshape(middle.shape)
    expert_gain_part = jnp.sum(grad_two * normed_two, axis=(0, 1))
    grad_middle = cotangent.astype(F32) + norm_backward(grad_two, expert_gain, normed_two, inverse_two)

    grad_flat = gather_tp(grad_middle.astype(BF16), 1).reshape(every, model_width)
    grad_attended = mm(grad_flat, output_full).astype(BF16)
    output_low = mm(grad_flat, attended, ((0,), (0,))).astype(BF16)
    output_grad = lax.psum_scatter(output_low, "fsdp", scatter_dimension=0, tiled=True).astype(F32)
    grad_pre, query_gain_part, key_gain_part = attend_back(
        pre, tables, gains, attended, grad_attended, rows, heads, kv_heads
    )
    qkv_low = mm(normed_rows, grad_pre, ((0,), (0,))).astype(BF16)
    qkv_grad = lax.psum_scatter(qkv_low, "fsdp", scatter_dimension=0, tiled=True).astype(F32)
    query_width, key_width = query_weight.shape[1], key_weight.shape[1]
    query_grad = qkv_grad[:, :query_width]
    key_grad = qkv_grad[:, query_width : query_width + key_width]
    value_grad = qkv_grad[:, query_width + key_width :]
    grad_normed = mm(grad_pre, qkv_full, ((1,), (1,))).reshape(rows, tp_size, local_length, model_width)
    grad_one = scatter_tp([grad_normed[:, j] for j in range(tp_size)])
    attention_gain_part = jnp.sum(grad_one * normed_one, axis=(0, 1))
    input_grad = grad_middle + norm_backward(grad_one, attention_gain, normed_one, inverse_one)

    weight_grads = []
    for kind in range(3):
        mine = jnp.stack([own_grads[e][kind] for e in range(local_experts)])
        far = [
            jnp.stack([far_grads[e][j][kind] for e in range(local_experts)])
            for j in range(tp_size - 1)
        ]
        weight_grads.append(scatter_tp([mine] + far))
    gate_grad, up_grad, down_grad = weight_grads

    router_grad = lax.psum_scatter(router_part, ("fsdp", "tp"), scatter_dimension=0, tiled=True)
    small = [
        lax.psum_scatter(value.reshape(-1), ("fsdp", "tp"), scatter_dimension=0, tiled=True)
        for value in (attention_gain_part, expert_gain_part, query_gain_part, key_gain_part)
    ]
    attention_gain_grad, expert_gain_grad, query_gain_grad, key_gain_grad = small
    return (
        layer_output,
        input_grad,
        attention_gain_grad,
        query_gain_grad,
        key_gain_grad,
        query_grad,
        key_grad,
        value_grad,
        output_grad,
        router_grad,
        expert_gain_grad,
        gate_grad,
        up_grad,
        down_grad,
    )


def solution(mesh):
    return jax.shard_map(
        local,
        mesh=mesh,
        in_specs=(
            P("fsdp", "tp", None),
            P(),
            P(),
            P(),
            P("fsdp", "tp"),
            P("fsdp", "tp"),
            P("fsdp", "tp"),
            P("fsdp", "tp"),
            P("fsdp", None),
            P(),
            P("fsdp", None, "tp"),
            P("fsdp", None, "tp"),
            P("fsdp", "tp", None),
            P("fsdp", None, None),
            P("fsdp", None),
            P("fsdp", "tp", None),
        ),
        out_specs=(
            P("fsdp", "tp", None),
            P("fsdp", "tp", None),
            P(("fsdp", "tp")),
            P(("fsdp", "tp")),
            P(("fsdp", "tp")),
            P("fsdp", "tp"),
            P("fsdp", "tp"),
            P("fsdp", "tp"),
            P("fsdp", "tp"),
            P(("fsdp", "tp"), None),
            P(("fsdp", "tp")),
            P("fsdp", None, "tp"),
            P("fsdp", None, "tp"),
            P("fsdp", "tp", None),
        ),
        check_vma=False,
    )
```

```python
import math

import jax
import jax.numpy as jnp
from jax import lax
from jax.experimental import pallas as pl
from jax.experimental.pallas import tpu as pltpu
from jax.sharding import PartitionSpec as P


EPSILON = 1e-06
ROPE_BASE = 1000000.0
NEGATIVE = -1e30
F32 = jnp.float32
BF16 = jnp.bfloat16


def inverse_rms(values):
    return lax.rsqrt(jnp.mean(values * values, axis=-1, keepdims=True) + EPSILON)


def norm_backward(grad_scaled, gain, normed, inverse):
    grad_normed = grad_scaled * gain
    return inverse * (grad_normed - normed * jnp.mean(grad_normed * normed, axis=-1, keepdims=True))


def mm(a, b, dims=((1,), (0,))):
    return lax.dot_general(a, b, (dims, ((), ())), preferred_element_type=F32)


def fetch_next(values, step):
    size = lax.axis_size("tp")
    return lax.ppermute(values, "tp", [(s, (s - step) % size) for s in range(size)])


def gather_tp(values, axis):
    size = lax.axis_size("tp")
    return jnp.concatenate([values] + [fetch_next(values, j) for j in range(1, size)], axis=axis)


def scatter_tp(pieces):
    size = lax.axis_size("tp")
    total = pieces[0].astype(F32)
    for j in range(1, size):
        moved = lax.ppermute(
            pieces[j].astype(BF16), "tp", [(s, (s + j) % size) for s in range(size)]
        )
        total = total + moved.astype(F32)
    return total


def chip_ring(nodes):
    chips = nodes // 2
    order = list(range(0, chips, 2)) + list(range(1, chips, 2))[::-1]
    links = [(order[i] * 2 + c, order[(i + 1) % chips] * 2 + c) for i in range(chips) for c in (0, 1)]
    swap = [(i, i ^ 1) for i in range(nodes)]
    return order, links, [(b, a) for a, b in links], swap


def ring_fits(nodes):
    return nodes % 4 == 0 and 8 <= nodes <= 16


def node_at(order, shift, core):
    place = jnp.asarray([order.index(i) for i in range(len(order))], jnp.int32)
    mine = place[lax.axis_index("fsdp") // 2]
    return jnp.asarray(order, jnp.int32)[(mine + shift) % len(order)] * 2 + core


def ring_gather(block, between):
    nodes = lax.axis_size("fsdp")
    if not ring_fits(nodes):
        for work in between:
            work(())
        return lax.all_gather(block, "fsdp", axis=0)
    order, up, down, swap = chip_ring(nodes)
    core = lax.axis_index("fsdp") % 2
    whole = jnp.zeros((nodes,) + block.shape, block.dtype)

    def keep(whole, piece, shift):
        other = lax.ppermute(piece, "fsdp", swap)
        for values, at in ((piece, core), (other, 1 - core)):
            whole = lax.dynamic_update_index_in_dim(whole, values, node_at(order, shift, at), 0)
        return whole

    whole = keep(whole, block, 0)
    ahead = behind = block
    for step in range(1, len(order) // 2 + 1):
        behind = lax.ppermute(behind, "fsdp", up)
        if step < (len(order) + 1) // 2:
            ahead = lax.ppermute(ahead, "fsdp", down)
        if step <= len(between):
            behind, ahead = between[step - 1]((behind, ahead))
        whole = keep(whole, behind, -step)
        if step < (len(order) + 1) // 2:
            whole = keep(whole, ahead, step)
    return whole


def ring_scatter(blocks):
    nodes = lax.axis_size("fsdp")
    if not ring_fits(nodes):
        return lax.psum_scatter(blocks, "fsdp", scatter_dimension=0, tiled=False).astype(F32)
    order, up, down, swap = chip_ring(nodes)
    core = lax.axis_index("fsdp") % 2

    def chip_sum(shift):
        mine = lax.dynamic_index_in_dim(blocks, node_at(order, shift, core), 0, keepdims=False)
        away = lax.dynamic_index_in_dim(blocks, node_at(order, shift, 1 - core), 0, keepdims=False)
        return mine.astype(F32) + lax.ppermute(away, "fsdp", swap).astype(F32)

    far = len(order) // 2
    rising = chip_sum(far).astype(BF16)
    falling = chip_sum(far + 1).astype(BF16)
    for step in range(far - 1, -1, -1):
        rising = lax.ppermute(rising, "fsdp", up).astype(F32)
        if step > 0:
            rising = (rising + chip_sum(step)).astype(BF16)
        if step < far - 1:
            falling = lax.ppermute(falling, "fsdp", down).astype(F32)
            if step > 0:
                falling = (falling + chip_sum(-step)).astype(BF16)
    return rising + falling + chip_sum(0)


def turn(values, cosine, sine):
    return values * cosine + pltpu.roll(values, values.shape[-1] // 2, 1) * sine


def turn_back(values, cosine, sine):
    return values * cosine - pltpu.roll(values, values.shape[-1] // 2, 1) * sine


def normed_turned(pre, gain, cosine, sine):
    inverse = inverse_rms(pre)
    normed = pre * inverse
    return inverse, normed, turn(normed * gain, cosine, sine).astype(BF16)


def weights_of(query_rot, key_rot, bias):
    factor = 1.0 / math.sqrt(query_rot.shape[-1])
    scores = mm(query_rot, key_rot, ((1,), (1,))) * factor + bias
    powers = jnp.exp(scores - jnp.max(scores, axis=-1, keepdims=True))
    return powers * (1.0 / jnp.sum(powers, axis=-1, keepdims=True))


def attend_kernel(q_ref, k_ref, v_ref, cos_ref, sin_ref, bias_ref, qg_ref, kg_ref, out_ref, key_rot):
    cosine, sine = cos_ref[...], sin_ref[...]

    @pl.when(pl.program_id(2) == 0)
    def _():
        key_rot[...] = normed_turned(k_ref[...], kg_ref[...], cosine, sine)[2]

    query_rot = normed_turned(q_ref[...], qg_ref[...], cosine, sine)[2]
    weights = weights_of(query_rot, key_rot[...], bias_ref[...])
    out_ref[...] = mm(weights.astype(BF16), v_ref[...].astype(BF16)).astype(BF16)


def attend_back_kernel(
    q_ref, k_ref, v_ref, cos_ref, sin_ref, bias_ref, qg_ref, kg_ref, att_ref, go_ref,
    grad_ref, qgain_ref, kgain_ref, key_rot, key_normed, key_inverse, grad_key, grad_value,
):
    row, kv, step = pl.program_id(0), pl.program_id(1), pl.program_id(2)
    group_size = pl.num_programs(2) - 2
    cosine, sine = cos_ref[...], sin_ref[...]
    factor = 1.0 / math.sqrt(q_ref.shape[-1])

    @pl.when((row == 0) & (kv == 0) & (step == 0))
    def _():
        qgain_ref[...] = jnp.zeros_like(qgain_ref)
        kgain_ref[...] = jnp.zeros_like(kgain_ref)

    @pl.when(step == 0)
    def _():
        inverse, normed, rotated = normed_turned(k_ref[...], kg_ref[...], cosine, sine)
        key_rot[...] = rotated
        key_normed[...] = normed
        key_inverse[...] = jnp.broadcast_to(inverse, key_inverse.shape)
        grad_key[...] = jnp.zeros_like(grad_key)
        grad_value[...] = jnp.zeros_like(grad_value)

    @pl.when(step < group_size)
    def _():
        inverse, normed, query_rot = normed_turned(q_ref[...], qg_ref[...], cosine, sine)
        weights = weights_of(query_rot, key_rot[...], bias_ref[...])
        grad_out = go_ref[...]
        grad_value[...] += mm(weights.astype(BF16), grad_out, ((0,), (0,)))
        grad_weights = mm(grad_out, v_ref[...].astype(BF16), ((1,), (1,)))
        delta = jnp.sum(att_ref[...].astype(F32) * grad_out.astype(F32), axis=-1, keepdims=True)
        grad_scores = (weights * (grad_weights - delta) * factor).astype(BF16)
        grad_query = turn_back(mm(grad_scores, key_rot[...]), cosine, sine)
        grad_key[...] += mm(grad_scores, query_rot, ((0,), (0,)))
        qgain_ref[...] += jnp.sum(grad_query * normed, axis=0, keepdims=True)
        grad_ref[...] = norm_backward(grad_query, qg_ref[...], normed, inverse).astype(BF16)

    @pl.when(step == group_size)
    def _():
        grad = turn_back(grad_key[...], cosine, sine)
        normed = key_normed[...]
        kgain_ref[...] += jnp.sum(grad * normed, axis=0, keepdims=True)
        grad_ref[...] = norm_backward(
            grad, kg_ref[...], normed, key_inverse[...][:, :1]
        ).astype(BF16)

    @pl.when(step == group_size + 1)
    def _():
        grad_ref[...] = grad_value[...].astype(BF16)


def attention_specs(length, head_size, heads, kv_heads):
    group_size = heads // kv_heads

    def head(r, kv, g):
        return (r, kv * group_size + jnp.minimum(g, group_size - 1))

    block = (length, head_size)
    full = pl.BlockSpec((1, head_size), lambda r, kv, g: (0, 0))
    return head, [
        pl.BlockSpec(block, head),
        pl.BlockSpec(block, lambda r, kv, g: (r, heads + kv)),
        pl.BlockSpec(block, lambda r, kv, g: (r, heads + kv_heads + kv)),
        pl.BlockSpec(block, lambda r, kv, g: (r, 0)),
        pl.BlockSpec(block, lambda r, kv, g: (r, 0)),
        pl.BlockSpec((None, length, length), lambda r, kv, g: (r, 0, 0)),
        full,
        full,
    ]


def attend(pre, tables, gains, rows, heads, kv_heads):
    length, head_size = pre.shape[0] // rows, gains[0].shape[1]
    head, specs = attention_specs(length, head_size, heads, kv_heads)
    cost = rows * heads * length * length
    return pl.pallas_call(
        attend_kernel,
        grid=(rows, kv_heads, heads // kv_heads),
        in_specs=specs,
        out_specs=pl.BlockSpec((length, head_size), head),
        out_shape=jax.ShapeDtypeStruct((pre.shape[0], heads * head_size), BF16),
        scratch_shapes=[pltpu.VMEM((length, head_size), BF16)],
        cost_estimate=pl.CostEstimate(
            flops=4 * cost * head_size, bytes_accessed=6 * pre.size, transcendentals=cost
        ),
        name="attend",
    )(pre, pre, pre, *tables, *gains)


def attend_back(pre, tables, gains, attended, grad_attended, rows, heads, kv_heads):
    length, head_size = pre.shape[0] // rows, gains[0].shape[1]
    group_size = heads // kv_heads
    head, specs = attention_specs(length, head_size, heads, kv_heads)

    def target(r, kv, g):
        own = kv * group_size + g
        return (r, jnp.where(g < group_size, own, heads + kv + jnp.where(g > group_size, kv_heads, 0)))

    block = pl.BlockSpec((length, head_size), head)
    full = pl.BlockSpec((1, head_size), lambda r, kv, g: (0, 0))
    gain = jax.ShapeDtypeStruct((1, head_size), F32)
    cost = rows * heads * length * length
    wide = pltpu.VMEM((length, head_size), F32)
    return pl.pallas_call(
        attend_back_kernel,
        grid=(rows, kv_heads, group_size + 2),
        in_specs=specs + [block, block],
        out_specs=[pl.BlockSpec((length, head_size), target), full, full],
        out_shape=[jax.ShapeDtypeStruct(pre.shape, BF16), gain, gain],
        scratch_shapes=[pltpu.VMEM((length, head_size), BF16), wide, wide, wide, wide],
        cost_estimate=pl.CostEstimate(
            flops=10 * cost * head_size, bytes_accessed=10 * pre.size, transcendentals=cost
        ),
        name="attend_back",
    )(pre, pre, pre, *tables, *gains, attended, grad_attended)


def layer(
    layer_input,
    attention_gain,
    query_gain,
    key_gain,
    query_weight,
    key_weight,
    value_weight,
    output_weight,
    router_weight,
    expert_gain,
    gate_weight,
    up_weight,
    down_weight,
    routes,
    segments,
    cotangent,
):
    rows, local_length, model_width = layer_input.shape
    length = segments.shape[1]
    head_size = query_gain.shape[0]
    expert_count = router_weight.shape[1]
    local_experts, _, half_hidden = gate_weight.shape
    top_count = routes.shape[2]
    nodes = lax.axis_size("fsdp")
    tp_size = lax.axis_size("tp")
    node = lax.axis_index("fsdp")
    part = lax.axis_index("tp")
    heads = query_weight.shape[1] // head_size
    kv_heads = key_weight.shape[1] // head_size
    capacity = max(2, rows * length * top_count * 5 // (4 * expert_count))
    tokens = rows * local_length
    places = min(capacity, tokens)
    every = tp_size * tokens

    qkv_full = lax.all_gather(
        jnp.concatenate([query_weight, key_weight, value_weight], axis=1), "fsdp", axis=0, tiled=True
    )
    input_wide = layer_input.astype(F32)
    inverse_one = inverse_rms(input_wide)
    normed_one = input_wide * inverse_one
    normed_low = (normed_one * attention_gain).astype(BF16)
    normed_rows = gather_tp(normed_low, 1).reshape(every, model_width)
    output_full = lax.all_gather(output_weight, "fsdp", axis=0, tiled=True)
    router_full = lax.all_gather(router_weight, "fsdp", axis=0, tiled=True)

    places_in = jnp.concatenate(
        [
            ((part + j) % tp_size) * local_length + jnp.arange(local_length, dtype=jnp.int32)
            for j in range(tp_size)
        ]
    )
    doubled = jnp.concatenate([segments, segments], axis=1)
    ids = lax.dynamic_slice_in_dim(doubled, part * local_length, length, axis=1)
    starts = jnp.sum((segments[:, None, :] < ids[:, :, None]).astype(jnp.int32), axis=2)
    half_size = head_size // 2
    frequency = jnp.exp(jnp.arange(half_size, dtype=F32) * (-2.0 * math.log(ROPE_BASE) / head_size))
    angles = (places_in[None, :] - starts).astype(F32)[:, :, None] * frequency
    cosine, sine = jnp.cos(angles), jnp.sin(angles)
    cosine_table = jnp.concatenate([cosine, cosine], axis=-1).reshape(every, head_size)
    sine_table = jnp.concatenate([-sine, sine], axis=-1).reshape(every, head_size)
    allowed = (ids[:, :, None] == ids[:, None, :]) & (places_in[None, :] <= places_in[:, None])[None]
    tables = (cosine_table, sine_table, jnp.where(allowed, 0.0, NEGATIVE).astype(F32))
    gains = (query_gain.reshape(1, head_size), key_gain.reshape(1, head_size))

    gate_weight, up_weight, down_weight, normed_rows = lax.optimization_barrier(
        (gate_weight, up_weight, down_weight, normed_rows)
    )
    gate_full = gather_tp(gate_weight, 2)
    up_full = gather_tp(up_weight, 2)
    down_full = gather_tp(down_weight, 1)

    own_routes = lax.dynamic_slice_in_dim(routes, part * local_length, local_length, axis=1)
    own_routes = own_routes.reshape(tokens, top_count)
    all_routes = lax.all_gather(own_routes, "fsdp", axis=0).reshape(nodes, tokens, top_count)
    own_experts = node * local_experts + jnp.arange(local_experts, dtype=jnp.int32)
    member = jnp.any(all_routes[:, None, :, :] == own_experts[None, :, None, None], axis=-1)
    before = jnp.arange(tokens)[:, None] < jnp.arange(tokens)[None, :]
    slot = jnp.einsum(
        "get,tu->geu", member.astype(BF16), before.astype(BF16), preferred_element_type=F32
    ).astype(jnp.int32)
    slot = jnp.where(member, slot, -1)
    placed = slot[:, :, None, :] == jnp.arange(places, dtype=jnp.int32)[None, None, :, None]

    normed_rows, router_full, all_routes = lax.optimization_barrier(
        (normed_rows, router_full, all_routes)
    )
    pre = mm(normed_rows, qkv_full)
    cot_low = cotangent.reshape(tokens, model_width)
    cot_low, pre = lax.optimization_barrier((cot_low, pre))
    attended = attend(pre, tables, gains, rows, heads, kv_heads)
    made = {}

    def project(moving):
        held, moving = lax.optimization_barrier((attended, moving))
        projected = mm(held, output_full, ((1,), (1,)))
        projected = projected.reshape(rows, tp_size, local_length, model_width)
        made["middle"] = input_wide + scatter_tp([projected[:, j] for j in range(tp_size)])
        return moving

    def settle(moving):
        made["middle"], moving = lax.optimization_barrier((made["middle"], moving))
        return moving

    cot_all = ring_gather(cot_low, (project, settle))
    middle = made["middle"]
    inverse_two = inverse_rms(middle)
    normed_two = middle * inverse_two
    expert_low = (normed_two * expert_gain).astype(BF16).reshape(tokens, model_width)

    rows_all = lax.all_gather(expert_low, "fsdp", axis=0)
    logits = mm(expert_low, router_full)
    chosen = jnp.any(
        own_routes[:, :, None] == jnp.arange(expert_count, dtype=jnp.int32), axis=1
    )
    top = jnp.max(jnp.where(chosen, logits, NEGATIVE), axis=-1, keepdims=True)
    powers = jnp.where(chosen, jnp.exp(jnp.minimum(logits - top, 0.0)), 0.0)
    gates = powers / jnp.sum(powers, axis=-1, keepdims=True)
    gates_out = jnp.moveaxis(gates.reshape(tokens, nodes, local_experts), 1, 0)
    own_gates = lax.all_to_all(gates_out, "fsdp", split_axis=0, concat_axis=0, tiled=True)
    gate_of = jnp.sum(
        jnp.where(placed, jnp.moveaxis(own_gates, 2, 1)[:, :, None, :], 0.0), axis=-1
    )

    out_total = None
    grad_total = None
    gate_columns = []
    own_grads = []
    far_grads = []
    for e in range(local_experts):
        spread = placed[:, e].astype(BF16)
        gate_here = gate_of[:, e].reshape(nodes * places, 1)
        arrived = jnp.einsum("gst,gtd->gsd", spread, rows_all, preferred_element_type=F32)
        arrived = arrived.astype(BF16).reshape(nodes * places, model_width)
        gate_pre = mm(arrived, gate_full[e])
        up_pre = mm(arrived, up_full[e])
        cots = jnp.einsum("gst,gtd->gsd", spread, cot_all, preferred_element_type=F32)
        cots = cots.astype(BF16).reshape(nodes * places, model_width)
        grad_plain = mm(cots, down_full[e], ((1,), (1,)))
        sigmoid_gate = jax.nn.sigmoid(gate_pre)
        activated = gate_pre * sigmoid_gate
        hidden = activated * up_pre
        gate_columns.append(jnp.sum(hidden * grad_plain, axis=-1).reshape(nodes, places))
        grad_hidden = grad_plain * gate_here
        grad_gate_pre = (
            grad_hidden * up_pre * sigmoid_gate * (1.0 + gate_pre * (1.0 - sigmoid_gate))
        ).astype(BF16)
        grad_up_pre = (grad_hidden * activated).astype(BF16)
        weighed = (hidden * gate_here).astype(BF16)
        grad_places = (
            mm(grad_gate_pre, gate_full[e], ((1,), (1,))) + mm(grad_up_pre, up_full[e], ((1,), (1,)))
        ).astype(BF16).reshape(nodes, places, model_width)
        produced = mm(weighed, down_full[e]).astype(BF16).reshape(nodes, places, model_width)
        out_here = jnp.einsum("gst,gsd->gtd", spread, produced, preferred_element_type=F32)
        grad_here = jnp.einsum("gst,gsd->gtd", spread, grad_places, preferred_element_type=F32)
        if out_total is not None:
            out_here = out_here + out_total.astype(F32)
            grad_here = grad_here + grad_total.astype(F32)
        out_total = out_here.astype(BF16)
        grad_total = grad_here.astype(BF16)
        grads = (
            mm(arrived, grad_gate_pre, ((0,), (0,))),
            mm(arrived, grad_up_pre, ((0,), (0,))),
            mm(weighed, cots, ((0,), (0,))),
        )
        own_grads.append(
            (grads[0][:, :half_hidden], grads[1][:, :half_hidden], grads[2][:half_hidden])
        )
        far_grads.append(
            [
                (
                    grads[0][:, j * half_hidden : (j + 1) * half_hidden].astype(BF16),
                    grads[1][:, j * half_hidden : (j + 1) * half_hidden].astype(BF16),
                    grads[2][j * half_hidden : (j + 1) * half_hidden].astype(BF16),
                )
                for j in range(1, tp_size)
            ]
        )

    column = jnp.sum(
        jnp.where(placed, jnp.stack(gate_columns, axis=1)[:, :, :, None], 0.0), axis=2
    )
    column = jnp.moveaxis(column, 1, 2)
    grad_gate = lax.all_to_all(column, "fsdp", split_axis=0, concat_axis=0, tiled=True)
    grad_gate = jnp.moveaxis(grad_gate, 0, 1).reshape(tokens, expert_count)

    grad_rows = ring_scatter(grad_total)
    expert_part = lax.psum_scatter(out_total, "fsdp", scatter_dimension=0, tiled=True)
    grad_rows, far_grads = lax.optimization_barrier((grad_rows, far_grads))
    grad_logits = (
        gates * (grad_gate - jnp.sum(gates * grad_gate, axis=-1, keepdims=True))
    ).astype(BF16)
    router_part = mm(expert_low, grad_logits, ((0,), (0,)))
    grad_two = grad_rows.reshape(tokens, model_width).astype(F32) + mm(
        grad_logits, router_full, ((1,), (1,))
    )
    grad_two = grad_two.reshape(middle.shape)
    expert_gain_part = jnp.sum(grad_two * normed_two, axis=(0, 1))
    grad_middle = cotangent.astype(F32) + norm_backward(grad_two, expert_gain, normed_two, inverse_two)

    grad_flat = gather_tp(grad_middle.astype(BF16), 1).reshape(every, model_width)
    grad_attended = mm(grad_flat, output_full).astype(BF16)
    output_low = mm(grad_flat, attended, ((0,), (0,))).astype(BF16)
    output_low, expert_part = lax.optimization_barrier((output_low, expert_part))
    output_part = lax.psum_scatter(output_low, "fsdp", scatter_dimension=0, tiled=True)
    grad_pre, query_gain_part, key_gain_part = attend_back(
        pre, tables, gains, attended, grad_attended, rows, heads, kv_heads
    )
    qkv_low = mm(normed_rows, grad_pre, ((0,), (0,))).astype(BF16)
    qkv_grad = ring_scatter(qkv_low.reshape(nodes, -1, qkv_low.shape[1]))
    qkv_grad = qkv_grad.reshape(query_weight.shape[0], -1)
    query_width, key_width = query_weight.shape[1], key_weight.shape[1]
    query_grad = qkv_grad[:, :query_width]
    key_grad = qkv_grad[:, query_width : query_width + key_width]
    value_grad = qkv_grad[:, query_width + key_width :]
    grad_normed = mm(grad_pre, qkv_full, ((1,), (1,))).reshape(rows, tp_size, local_length, model_width)
    grad_one = scatter_tp([grad_normed[:, j] for j in range(tp_size)])
    attention_gain_part = jnp.sum(grad_one * normed_one, axis=(0, 1))
    input_grad = grad_middle + norm_backward(grad_one, attention_gain, normed_one, inverse_one)

    weight_grads = []
    for kind in range(3):
        mine = jnp.stack([own_grads[e][kind] for e in range(local_experts)])
        far = [
            jnp.stack([far_grads[e][j][kind] for e in range(local_experts)])
            for j in range(tp_size - 1)
        ]
        weight_grads.append(scatter_tp([mine] + far))
    gate_grad, up_grad, down_grad = weight_grads

    layer_output = (middle + expert_part.reshape(middle.shape).astype(F32)).astype(BF16)
    router_part, output_part = lax.optimization_barrier((router_part, output_part))
    router_grad = lax.psum_scatter(router_part, ("fsdp", "tp"), scatter_dimension=0, tiled=True)
    output_grad = output_part.astype(F32)
    small = [
        lax.psum_scatter(value.reshape(-1), ("fsdp", "tp"), scatter_dimension=0, tiled=True)
        for value in (attention_gain_part, expert_gain_part, query_gain_part, key_gain_part)
    ]
    attention_gain_grad, expert_gain_grad, query_gain_grad, key_gain_grad = small
    return (
        layer_output,
        input_grad,
        attention_gain_grad,
        query_gain_grad,
        key_gain_grad,
        query_grad,
        key_grad,
        value_grad,
        output_grad,
        router_grad,
        expert_gain_grad,
        gate_grad,
        up_grad,
        down_grad,
    )


def solution(mesh):
    return jax.shard_map(
        layer,
        mesh=mesh,
        in_specs=(
            P("fsdp", "tp", None),
            P(),
            P(),
            P(),
            P("fsdp", "tp"),
            P("fsdp", "tp"),
            P("fsdp", "tp"),
            P("fsdp", "tp"),
            P("fsdp", None),
            P(),
            P("fsdp", None, "tp"),
            P("fsdp", None, "tp"),
            P("fsdp", "tp", None),
            P("fsdp", None, None),
            P("fsdp", None),
            P("fsdp", "tp", None),
        ),
        out_specs=(
            P("fsdp", "tp", None),
            P("fsdp", "tp", None),
            P(("fsdp", "tp")),
            P(("fsdp", "tp")),
            P(("fsdp", "tp")),
            P("fsdp", "tp"),
            P("fsdp", "tp"),
            P("fsdp", "tp"),
            P("fsdp", "tp"),
            P(("fsdp", "tp"), None),
            P(("fsdp", "tp")),
            P("fsdp", None, "tp"),
            P("fsdp", None, "tp"),
            P("fsdp", "tp", None),
        ),
        check_vma=False,
    )
```

```python
import functools
import math

import jax
import jax.numpy as jnp
from jax import lax
from jax.experimental import pallas as pl
from jax.experimental.pallas import tpu as pltpu
from jax.sharding import PartitionSpec as P


EPSILON = 1e-06
ROPE_BASE = 1000000.0
NEGATIVE = -1e30
F32 = jnp.float32
BF16 = jnp.bfloat16


def inverse_rms(values):
    return lax.rsqrt(jnp.mean(values * values, axis=-1, keepdims=True) + EPSILON)


def norm_backward(grad_scaled, gain, normed, inverse):
    grad_normed = grad_scaled * gain
    return inverse * (grad_normed - normed * jnp.mean(grad_normed * normed, axis=-1, keepdims=True))


def mm(a, b, dims=((1,), (0,))):
    return lax.dot_general(a, b, (dims, ((), ())), preferred_element_type=F32)


def fetch_next(values, step):
    size = lax.axis_size("tp")
    return lax.ppermute(values, "tp", [(s, (s - step) % size) for s in range(size)])


def gather_tp(values, axis):
    size = lax.axis_size("tp")
    return jnp.concatenate([values] + [fetch_next(values, j) for j in range(1, size)], axis=axis)


def scatter_tp(pieces):
    size = lax.axis_size("tp")
    total = pieces[0].astype(F32)
    for j in range(1, size):
        moved = lax.ppermute(
            pieces[j].astype(BF16), "tp", [(s, (s + j) % size) for s in range(size)]
        )
        total = total + moved.astype(F32)
    return total


def chip_ring(nodes):
    chips = nodes // 2
    order = list(range(0, chips, 2)) + list(range(1, chips, 2))[::-1]
    links = [(order[i] * 2 + c, order[(i + 1) % chips] * 2 + c) for i in range(chips) for c in (0, 1)]
    swap = [(i, i ^ 1) for i in range(nodes)]
    return order, links, [(b, a) for a, b in links], swap


def ring_fits(nodes):
    return nodes % 4 == 0 and 8 <= nodes <= 16


def node_at(order, shift, core):
    place = jnp.asarray([order.index(i) for i in range(len(order))], jnp.int32)
    mine = place[lax.axis_index("fsdp") // 2]
    return jnp.asarray(order, jnp.int32)[(mine + shift) % len(order)] * 2 + core


def ring_gather(block, between):
    nodes = lax.axis_size("fsdp")
    if not ring_fits(nodes):
        for work in between:
            work(())
        return lax.all_gather(block, "fsdp", axis=0)
    order, up, down, swap = chip_ring(nodes)
    core = lax.axis_index("fsdp") % 2
    whole = jnp.zeros((nodes,) + block.shape, block.dtype)

    def keep(whole, piece, shift):
        other = lax.ppermute(piece, "fsdp", swap)
        for values, at in ((piece, core), (other, 1 - core)):
            whole = lax.dynamic_update_index_in_dim(whole, values, node_at(order, shift, at), 0)
        return whole

    whole = keep(whole, block, 0)
    ahead = behind = block
    for step in range(1, len(order) // 2 + 1):
        behind = lax.ppermute(behind, "fsdp", up)
        if step < (len(order) + 1) // 2:
            ahead = lax.ppermute(ahead, "fsdp", down)
        if step <= len(between):
            behind, ahead = between[step - 1]((behind, ahead))
        whole = keep(whole, behind, -step)
        if step < (len(order) + 1) // 2:
            whole = keep(whole, ahead, step)
    return whole


def ring_scatter(blocks):
    nodes = lax.axis_size("fsdp")
    if not ring_fits(nodes):
        return lax.psum_scatter(blocks, "fsdp", scatter_dimension=0, tiled=False).astype(F32)
    order, up, down, swap = chip_ring(nodes)
    core = lax.axis_index("fsdp") % 2

    def chip_sum(shift):
        mine = lax.dynamic_index_in_dim(blocks, node_at(order, shift, core), 0, keepdims=False)
        away = lax.dynamic_index_in_dim(blocks, node_at(order, shift, 1 - core), 0, keepdims=False)
        return mine.astype(F32) + lax.ppermute(away, "fsdp", swap).astype(F32)

    far = len(order) // 2
    rising = chip_sum(far).astype(BF16)
    falling = chip_sum(far + 1).astype(BF16)
    for step in range(far - 1, -1, -1):
        rising = lax.ppermute(rising, "fsdp", up).astype(F32)
        if step > 0:
            rising = (rising + chip_sum(step)).astype(BF16)
        if step < far - 1:
            falling = lax.ppermute(falling, "fsdp", down).astype(F32)
            if step > 0:
                falling = (falling + chip_sum(-step)).astype(BF16)
    return rising + falling + chip_sum(0)


def turn(values, cosine, sine):
    return values * cosine + pltpu.roll(values, values.shape[-1] // 2, 1) * sine


def turn_back(values, cosine, sine):
    return values * cosine - pltpu.roll(values, values.shape[-1] // 2, 1) * sine


def normed_turned(pre, gain, cosine, sine):
    inverse = inverse_rms(pre)
    normed = pre * inverse
    return inverse, normed, turn(normed * gain, cosine, sine).astype(BF16)


def weights_of(query_rot, key_rot, bias):
    factor = 1.0 / math.sqrt(query_rot.shape[-1])
    scores = mm(query_rot, key_rot, ((1,), (1,))) * factor + bias
    powers = jnp.exp(scores - jnp.max(scores, axis=-1, keepdims=True))
    return powers * (1.0 / jnp.sum(powers, axis=-1, keepdims=True))


def attend_kernel(q_ref, k_ref, v_ref, cos_ref, sin_ref, bias_ref, qg_ref, kg_ref, out_ref, key_rot):
    cosine, sine = cos_ref[...], sin_ref[...]

    @pl.when(pl.program_id(2) == 0)
    def _():
        key_rot[...] = normed_turned(k_ref[...], kg_ref[...], cosine, sine)[2]

    query_rot = normed_turned(q_ref[...], qg_ref[...], cosine, sine)[2]
    weights = weights_of(query_rot, key_rot[...], bias_ref[...])
    out_ref[...] = mm(weights.astype(BF16), v_ref[...].astype(BF16)).astype(BF16)


def attend_back_kernel(
    q_ref, k_ref, v_ref, cos_ref, sin_ref, bias_ref, qg_ref, kg_ref, att_ref, go_ref,
    grad_ref, qgain_ref, kgain_ref, key_rot, key_normed, key_inverse, grad_key, grad_value,
):
    row, kv, step = pl.program_id(0), pl.program_id(1), pl.program_id(2)
    group_size = pl.num_programs(2) - 2
    cosine, sine = cos_ref[...], sin_ref[...]
    factor = 1.0 / math.sqrt(q_ref.shape[-1])

    @pl.when((row == 0) & (kv == 0) & (step == 0))
    def _():
        qgain_ref[...] = jnp.zeros_like(qgain_ref)
        kgain_ref[...] = jnp.zeros_like(kgain_ref)

    @pl.when(step == 0)
    def _():
        inverse, normed, rotated = normed_turned(k_ref[...], kg_ref[...], cosine, sine)
        key_rot[...] = rotated
        key_normed[...] = normed
        key_inverse[...] = jnp.broadcast_to(inverse, key_inverse.shape)
        grad_key[...] = jnp.zeros_like(grad_key)
        grad_value[...] = jnp.zeros_like(grad_value)

    @pl.when(step < group_size)
    def _():
        inverse, normed, query_rot = normed_turned(q_ref[...], qg_ref[...], cosine, sine)
        weights = weights_of(query_rot, key_rot[...], bias_ref[...])
        grad_out = go_ref[...]
        grad_value[...] += mm(weights.astype(BF16), grad_out, ((0,), (0,)))
        grad_weights = mm(grad_out, v_ref[...].astype(BF16), ((1,), (1,)))
        delta = jnp.sum(att_ref[...].astype(F32) * grad_out.astype(F32), axis=-1, keepdims=True)
        grad_scores = (weights * (grad_weights - delta) * factor).astype(BF16)
        grad_query = turn_back(mm(grad_scores, key_rot[...]), cosine, sine)
        grad_key[...] += mm(grad_scores, query_rot, ((0,), (0,)))
        qgain_ref[...] += jnp.sum(grad_query * normed, axis=0, keepdims=True)
        grad_ref[...] = norm_backward(grad_query, qg_ref[...], normed, inverse).astype(BF16)

    @pl.when(step == group_size)
    def _():
        grad = turn_back(grad_key[...], cosine, sine)
        normed = key_normed[...]
        kgain_ref[...] += jnp.sum(grad * normed, axis=0, keepdims=True)
        grad_ref[...] = norm_backward(
            grad, kg_ref[...], normed, key_inverse[...][:, :1]
        ).astype(BF16)

    @pl.when(step == group_size + 1)
    def _():
        grad_ref[...] = grad_value[...].astype(BF16)


def attention_specs(length, head_size, heads, kv_heads):
    group_size = heads // kv_heads

    def head(r, kv, g):
        return (r, kv * group_size + jnp.minimum(g, group_size - 1))

    block = (length, head_size)
    full = pl.BlockSpec((1, head_size), lambda r, kv, g: (0, 0))
    return head, [
        pl.BlockSpec(block, head),
        pl.BlockSpec(block, lambda r, kv, g: (r, heads + kv)),
        pl.BlockSpec(block, lambda r, kv, g: (r, heads + kv_heads + kv)),
        pl.BlockSpec(block, lambda r, kv, g: (r, 0)),
        pl.BlockSpec(block, lambda r, kv, g: (r, 0)),
        pl.BlockSpec((None, length, length), lambda r, kv, g: (r, 0, 0)),
        full,
        full,
    ]


def attend(pre, tables, gains, rows, heads, kv_heads):
    length, head_size = pre.shape[0] // rows, gains[0].shape[1]
    head, specs = attention_specs(length, head_size, heads, kv_heads)
    cost = rows * heads * length * length
    return pl.pallas_call(
        attend_kernel,
        grid=(rows, kv_heads, heads // kv_heads),
        in_specs=specs,
        out_specs=pl.BlockSpec((length, head_size), head),
        out_shape=jax.ShapeDtypeStruct((pre.shape[0], heads * head_size), BF16),
        scratch_shapes=[pltpu.VMEM((length, head_size), BF16)],
        cost_estimate=pl.CostEstimate(
            flops=4 * cost * head_size, bytes_accessed=6 * pre.size, transcendentals=cost
        ),
        name="attend",
    )(pre, pre, pre, *tables, *gains)


def attend_back(pre, tables, gains, attended, grad_attended, rows, heads, kv_heads):
    length, head_size = pre.shape[0] // rows, gains[0].shape[1]
    group_size = heads // kv_heads
    head, specs = attention_specs(length, head_size, heads, kv_heads)

    def target(r, kv, g):
        own = kv * group_size + g
        return (r, jnp.where(g < group_size, own, heads + kv + jnp.where(g > group_size, kv_heads, 0)))

    block = pl.BlockSpec((length, head_size), head)
    full = pl.BlockSpec((1, head_size), lambda r, kv, g: (0, 0))
    gain = jax.ShapeDtypeStruct((1, head_size), F32)
    cost = rows * heads * length * length
    wide = pltpu.VMEM((length, head_size), F32)
    return pl.pallas_call(
        attend_back_kernel,
        grid=(rows, kv_heads, group_size + 2),
        in_specs=specs + [block, block],
        out_specs=[pl.BlockSpec((length, head_size), target), full, full],
        out_shape=[jax.ShapeDtypeStruct(pre.shape, BF16), gain, gain],
        scratch_shapes=[pltpu.VMEM((length, head_size), BF16), wide, wide, wide, wide],
        cost_estimate=pl.CostEstimate(
            flops=10 * cost * head_size, bytes_accessed=10 * pre.size, transcendentals=cost
        ),
        name="attend_back",
    )(pre, pre, pre, *tables, *gains, attended, grad_attended)


TILE = 256
PACK = 16
GRANT = 60 * 1024 * 1024
HELD = 20 * 1024 * 1024


def pick_kernel(tiles, first, last, places_ref, rows_ref, out_ref, total):
    e, j = pl.program_id(1), pl.program_id(2)

    @pl.when(j < tiles[e])
    def _():
        total[...] = jnp.zeros_like(total)
        at = e * pl.num_programs(2) + j
        wanted = j * TILE + lax.broadcasted_iota(jnp.int32, (TILE, places_ref.shape[2]), 0)

        def add(g, carry):
            hits = jnp.where(places_ref[g] == wanted, 1.0, 0.0).astype(BF16)
            total[...] += mm(hits, rows_ref[g])
            return carry

        lax.fori_loop(first[at], last[at] + 1, add, 0)
        out_ref[...] = total[...].astype(BF16)

    @pl.when(j >= tiles[e])
    def _():
        out_ref[...] = jnp.zeros_like(out_ref)


def pick(plan, source, start, width):
    experts, nodes, _, tokens = plan["places"].shape
    count = plan["tile_count"]
    cuts = 1
    while 2 * nodes * tokens * (width // cuts) > HELD and width % (256 * cuts) == 0:
        cuts *= 2
    part = width // cuts
    return pl.pallas_call(
        pick_kernel,
        grid_spec=pltpu.PrefetchScalarGridSpec(
            num_scalar_prefetch=3,
            grid=(cuts, experts, count),
            in_specs=[
                pl.BlockSpec((None, nodes, 1, tokens), lambda c, e, j, *_: (e, 0, 0, 0)),
                pl.BlockSpec(
                    (nodes, tokens, part),
                    lambda c, e, j, *_: (0, 0, start // part + c),
                    pipeline_mode=pl.Buffered(1),
                ),
            ],
            out_specs=pl.BlockSpec((None, TILE, part), lambda c, e, j, *_: (e, j, c)),
            scratch_shapes=[pltpu.VMEM((TILE, part), F32)],
        ),
        out_shape=jax.ShapeDtypeStruct((experts, count * TILE, width), BF16),
        compiler_params=pltpu.CompilerParams(vmem_limit_bytes=GRANT),
        cost_estimate=pl.CostEstimate(
            flops=6 * experts * count * TILE * tokens * width,
            bytes_accessed=2 * nodes * tokens * width + 2 * experts * count * TILE * width,
            transcendentals=0,
        ),
        name="pick",
    )(plan["tiles"], plan["first"], plan["last"], plan["places"], source)


def expert_kernel(
    tiles, base, arrived_ref, extra_ref, cots_ref, gate_ref, up_ref, down_ref,
    weighed_ref, grad_gate_ref, grad_up_ref, produced_ref, back_ref, column_ref, *, expert_count,
):
    e, j = pl.program_id(0), pl.program_id(1)

    @pl.when(j < tiles[e])
    def _():
        lane = lax.broadcasted_iota(jnp.int32, extra_ref.shape, 1)
        own = base[0] + e
        gates = jnp.where(
            (lane == own) | (lane == own + expert_count), extra_ref[...].astype(F32), 0.0
        )
        gate_here = jnp.sum(gates, axis=-1, keepdims=True)
        gate_pre = mm(arrived_ref[...], gate_ref[...])
        up_pre = mm(arrived_ref[...], up_ref[...])
        grad_plain = mm(cots_ref[...], down_ref[...], ((1,), (1,)))
        sigmoid_gate = 1.0 / (1.0 + jnp.exp(-gate_pre))
        activated = gate_pre * sigmoid_gate
        hidden = activated * up_pre
        column = jnp.sum(hidden * grad_plain, axis=-1, keepdims=True)
        high = column.astype(BF16).astype(F32)
        spot = lax.broadcasted_iota(jnp.int32, column_ref.shape, 1)
        column_ref[...] = jnp.where(
            spot == 2 * e, high, jnp.where(spot == 2 * e + 1, column - high, 0.0)
        ).astype(BF16)
        weighed = (hidden * gate_here).astype(BF16)
        weighed_ref[...] = weighed
        grad_hidden = grad_plain * gate_here
        grad_gate = (
            grad_hidden * up_pre * sigmoid_gate * (1.0 + gate_pre * (1.0 - sigmoid_gate))
        ).astype(BF16)
        grad_up = (grad_hidden * activated).astype(BF16)
        grad_gate_ref[...] = grad_gate
        grad_up_ref[...] = grad_up
        produced_ref[...] = mm(weighed, down_ref[...]).astype(BF16)
        back_ref[...] = (
            mm(grad_gate, gate_ref[...], ((1,), (1,))) + mm(grad_up, up_ref[...], ((1,), (1,)))
        ).astype(BF16)

    @pl.when(j >= tiles[e])
    def _():
        for ref in (weighed_ref, grad_gate_ref, grad_up_ref, produced_ref, back_ref, column_ref):
            ref[...] = jnp.zeros_like(ref)


def run_experts(plan, base, arrived, extra, cots, gate, up, down, expert_count):
    experts, height, width = arrived.shape
    hidden = gate.shape[2]
    count = plan["tile_count"]

    def tile(size):
        return pl.BlockSpec((None, TILE, size), lambda e, j, *_: (e, j, 0))

    def whole(shape):
        return pl.BlockSpec((None,) + shape, lambda e, j, *_: (e, 0, 0))

    def out(size):
        return jax.ShapeDtypeStruct((experts, height, size), BF16)

    return pl.pallas_call(
        functools.partial(expert_kernel, expert_count=expert_count),
        grid_spec=pltpu.PrefetchScalarGridSpec(
            num_scalar_prefetch=2,
            grid=(experts, count),
            in_specs=[
                tile(width), tile(extra.shape[2]), tile(width),
                whole((width, hidden)), whole((width, hidden)), whole((hidden, width)),
            ],
            out_specs=[tile(hidden)] * 3 + [tile(width)] * 2 + [tile(128)],
        ),
        out_shape=[out(hidden)] * 3 + [out(width)] * 2 + [out(128)],
        compiler_params=pltpu.CompilerParams(vmem_limit_bytes=GRANT),
        cost_estimate=pl.CostEstimate(
            flops=6 * experts * height * width * hidden,
            bytes_accessed=2 * experts * (4 * height * width + 3 * height * hidden),
            transcendentals=experts * height * hidden // 2,
        ),
        name="run_experts",
    )(plan["tiles"], base, arrived, extra, cots, gate, up, down)


def spread_kernel(starts, places_ref, *refs):
    g = pl.program_id(0)
    half = len(refs) // 2
    experts, nodes = places_ref.shape[0], pl.num_programs(0)
    window = refs[-1]
    size = window.shape[0]
    totals = [None] * half
    for e in range(experts):
        start = pl.multiple_of(starts[e * nodes + g], PACK)
        wanted = start + lax.broadcasted_iota(jnp.int32, (size, places_ref.shape[2]), 0)
        hits = jnp.where(places_ref[e] == wanted, 1.0, 0.0).astype(BF16)
        for i in range(half):
            part = mm(hits, refs[i][e, pl.ds(start, size), :], ((0,), (0,)))
            totals[i] = part if totals[i] is None else totals[i] + part
    for i in range(half):
        refs[half + i][...] = totals[i].astype(BF16)


def spread(plan, sources):
    experts, nodes, _, tokens = plan["places"].shape
    window = plan["window"]
    return pl.pallas_call(
        spread_kernel,
        grid_spec=pltpu.PrefetchScalarGridSpec(
            num_scalar_prefetch=1,
            grid=(nodes,),
            in_specs=[pl.BlockSpec((experts, None, 1, tokens), lambda g, *_: (0, g, 0, 0))]
            + [
                pl.BlockSpec(source.shape, lambda g, *_: (0, 0, 0), pipeline_mode=pl.Buffered(1))
                for source in sources
            ],
            out_specs=[
                pl.BlockSpec((None, tokens, source.shape[2]), lambda g, *_: (g, 0, 0))
                for source in sources
            ],
            scratch_shapes=[pltpu.VMEM((window, 128), BF16)],
        ),
        out_shape=[
            jax.ShapeDtypeStruct((nodes, tokens, source.shape[2]), BF16) for source in sources
        ],
        compiler_params=pltpu.CompilerParams(vmem_limit_bytes=GRANT),
        cost_estimate=pl.CostEstimate(
            flops=2 * experts * nodes * tokens * window * sum(s.shape[2] for s in sources),
            bytes_accessed=sum(4 * s.size for s in sources),
            transcendentals=0,
        ),
        name="spread",
    )(plan["starts"], plan["places"], *sources)


def plan_places(member, slot, places):
    nodes, _, _ = member.shape
    counts = jnp.sum(member.astype(jnp.int32), axis=2)
    earlier = jnp.arange(nodes)[:, None] > jnp.arange(nodes)[None, :]
    offset = jnp.sum(jnp.where(earlier[:, :, None], counts[None], 0), axis=1)
    totals = jnp.sum(counts, axis=0)
    count = -(-(nodes * places) // TILE)
    edges = jnp.arange(count, dtype=jnp.int32) * TILE
    ends = offset + counts
    first = jnp.sum((ends[:, :, None] <= edges).astype(jnp.int32), axis=0)
    last = jnp.sum((offset[:, :, None] < edges + TILE).astype(jnp.int32), axis=0) - 1
    window = -(-places // PACK) * PACK + PACK
    window = min(window, count * TILE)
    starts = jnp.minimum(offset // PACK * PACK, count * TILE - window)
    packed = jnp.where(member, offset[:, :, None] + slot, -1)
    return {
        "places": jnp.moveaxis(packed, 1, 0)[:, :, None, :],
        "tiles": (totals + TILE - 1) // TILE,
        "first": jnp.minimum(first, nodes - 1).reshape(-1),
        "last": jnp.minimum(last, nodes - 1).reshape(-1),
        "starts": starts.T.reshape(-1),
        "tile_count": count,
        "window": window,
    }


def layer(
    layer_input,
    attention_gain,
    query_gain,
    key_gain,
    query_weight,
    key_weight,
    value_weight,
    output_weight,
    router_weight,
    expert_gain,
    gate_weight,
    up_weight,
    down_weight,
    routes,
    segments,
    cotangent,
):
    rows, local_length, model_width = layer_input.shape
    length = segments.shape[1]
    head_size = query_gain.shape[0]
    expert_count = router_weight.shape[1]
    local_experts, _, half_hidden = gate_weight.shape
    top_count = routes.shape[2]
    nodes = lax.axis_size("fsdp")
    tp_size = lax.axis_size("tp")
    node = lax.axis_index("fsdp")
    part = lax.axis_index("tp")
    heads = query_weight.shape[1] // head_size
    kv_heads = key_weight.shape[1] // head_size
    capacity = max(2, rows * length * top_count * 5 // (4 * expert_count))
    tokens = rows * local_length
    places = min(capacity, tokens)
    every = tp_size * tokens

    qkv_full = lax.all_gather(
        jnp.concatenate([query_weight, key_weight, value_weight], axis=1), "fsdp", axis=0, tiled=True
    )
    input_wide = layer_input.astype(F32)
    inverse_one = inverse_rms(input_wide)
    normed_one = input_wide * inverse_one
    normed_low = (normed_one * attention_gain).astype(BF16)
    normed_rows = gather_tp(normed_low, 1).reshape(every, model_width)
    output_full = lax.all_gather(output_weight, "fsdp", axis=0, tiled=True)
    router_full = lax.all_gather(router_weight, "fsdp", axis=0, tiled=True)

    places_in = jnp.concatenate(
        [
            ((part + j) % tp_size) * local_length + jnp.arange(local_length, dtype=jnp.int32)
            for j in range(tp_size)
        ]
    )
    doubled = jnp.concatenate([segments, segments], axis=1)
    ids = lax.dynamic_slice_in_dim(doubled, part * local_length, length, axis=1)
    starts = jnp.sum((segments[:, None, :] < ids[:, :, None]).astype(jnp.int32), axis=2)
    half_size = head_size // 2
    frequency = jnp.exp(jnp.arange(half_size, dtype=F32) * (-2.0 * math.log(ROPE_BASE) / head_size))
    angles = (places_in[None, :] - starts).astype(F32)[:, :, None] * frequency
    cosine, sine = jnp.cos(angles), jnp.sin(angles)
    cosine_table = jnp.concatenate([cosine, cosine], axis=-1).reshape(every, head_size)
    sine_table = jnp.concatenate([-sine, sine], axis=-1).reshape(every, head_size)
    allowed = (ids[:, :, None] == ids[:, None, :]) & (places_in[None, :] <= places_in[:, None])[None]
    tables = (cosine_table, sine_table, jnp.where(allowed, 0.0, NEGATIVE).astype(F32))
    gains = (query_gain.reshape(1, head_size), key_gain.reshape(1, head_size))

    gate_weight, up_weight, down_weight, normed_rows = lax.optimization_barrier(
        (gate_weight, up_weight, down_weight, normed_rows)
    )
    gate_full = gather_tp(gate_weight, 2)
    up_full = gather_tp(up_weight, 2)

    own_routes = lax.dynamic_slice_in_dim(routes, part * local_length, local_length, axis=1)
    own_routes = own_routes.reshape(tokens, top_count)
    all_routes = lax.all_gather(own_routes, "fsdp", axis=0).reshape(nodes, tokens, top_count)
    own_experts = node * local_experts + jnp.arange(local_experts, dtype=jnp.int32)
    member = jnp.any(all_routes[:, None, :, :] == own_experts[None, :, None, None], axis=-1)
    before = jnp.arange(tokens)[:, None] < jnp.arange(tokens)[None, :]
    slot = jnp.einsum(
        "get,tu->geu", member.astype(BF16), before.astype(BF16), preferred_element_type=F32
    ).astype(jnp.int32)
    plan = plan_places(member, slot, places)
    base = (node * local_experts).reshape(1).astype(jnp.int32)

    normed_rows, router_full, all_routes = lax.optimization_barrier(
        (normed_rows, router_full, all_routes)
    )
    pre = mm(normed_rows, qkv_full)
    cot_low = cotangent.reshape(tokens, model_width)
    cot_low, pre = lax.optimization_barrier((cot_low, pre))
    attended = attend(pre, tables, gains, rows, heads, kv_heads)
    made = {}

    def project(moving):
        held, moving = lax.optimization_barrier((attended, moving))
        projected = mm(held, output_full, ((1,), (1,)))
        projected = projected.reshape(rows, tp_size, local_length, model_width)
        made["middle"] = input_wide + scatter_tp([projected[:, j] for j in range(tp_size)])
        return moving

    cot_all = ring_gather(cot_low, (project,))
    middle, down_weight = lax.optimization_barrier((made["middle"], down_weight))
    down_full = gather_tp(down_weight, 1)
    inverse_two = inverse_rms(middle)
    normed_two = middle * inverse_two
    expert_low = (normed_two * expert_gain).astype(BF16).reshape(tokens, model_width)

    logits = mm(expert_low, router_full)
    chosen = jnp.any(
        own_routes[:, :, None] == jnp.arange(expert_count, dtype=jnp.int32), axis=1
    )
    top = jnp.max(jnp.where(chosen, logits, NEGATIVE), axis=-1, keepdims=True)
    powers = jnp.where(chosen, jnp.exp(jnp.minimum(logits - top, 0.0)), 0.0)
    gates = powers / jnp.sum(powers, axis=-1, keepdims=True)
    high = lax.reduce_precision(gates, 8, 7)
    filler = jnp.zeros((tokens, -2 * expert_count % 128), BF16)
    sent = jnp.concatenate(
        [expert_low, high.astype(BF16), (gates - high).astype(BF16), filler], axis=1
    )
    rows_all = lax.all_gather(sent, "fsdp", axis=0)

    arrived = pick(plan, rows_all, 0, model_width)
    extra = pick(plan, rows_all, model_width, sent.shape[1] - model_width)
    cots = pick(plan, cot_all, 0, model_width)
    weighed, grad_gate_pre, grad_up_pre, produced, back, columns = run_experts(
        plan, base, arrived, extra, cots, gate_full, up_full, down_full, expert_count
    )
    out_total = spread(plan, [produced])[0]
    out_total, back = lax.optimization_barrier((out_total, back))
    grad_total, columns = spread(plan, [back, columns])
    own_grads = []
    far_grads = []
    for e in range(local_experts):
        grads = (
            mm(arrived[e], grad_gate_pre[e], ((0,), (0,))),
            mm(arrived[e], grad_up_pre[e], ((0,), (0,))),
            mm(weighed[e], cots[e], ((0,), (0,))),
        )
        own_grads.append(
            (grads[0][:, :half_hidden], grads[1][:, :half_hidden], grads[2][:half_hidden])
        )
        far_grads.append(
            [
                (
                    grads[0][:, j * half_hidden : (j + 1) * half_hidden].astype(BF16),
                    grads[1][:, j * half_hidden : (j + 1) * half_hidden].astype(BF16),
                    grads[2][j * half_hidden : (j + 1) * half_hidden].astype(BF16),
                )
                for j in range(1, tp_size)
            ]
        )

    pairs = columns[:, :, : 2 * local_experts].astype(F32).reshape(nodes, tokens, local_experts, 2)
    column = jnp.sum(pairs, axis=-1)
    grad_gate = lax.all_to_all(column, "fsdp", split_axis=0, concat_axis=0, tiled=True)
    grad_gate = jnp.moveaxis(grad_gate, 0, 1).reshape(tokens, expert_count)

    grad_rows = ring_scatter(grad_total)
    expert_part = lax.psum_scatter(out_total, "fsdp", scatter_dimension=0, tiled=True)
    grad_rows, far_grads = lax.optimization_barrier((grad_rows, far_grads))
    grad_logits = (
        gates * (grad_gate - jnp.sum(gates * grad_gate, axis=-1, keepdims=True))
    ).astype(BF16)
    router_part = mm(expert_low, grad_logits, ((0,), (0,)))
    grad_two = grad_rows.reshape(tokens, model_width).astype(F32) + mm(
        grad_logits, router_full, ((1,), (1,))
    )
    grad_two = grad_two.reshape(middle.shape)
    expert_gain_part = jnp.sum(grad_two * normed_two, axis=(0, 1))
    grad_middle = cotangent.astype(F32) + norm_backward(grad_two, expert_gain, normed_two, inverse_two)

    grad_flat = gather_tp(grad_middle.astype(BF16), 1).reshape(every, model_width)
    grad_attended = mm(grad_flat, output_full).astype(BF16)
    output_low = mm(grad_flat, attended, ((0,), (0,))).astype(BF16)
    output_low, grad_attended = lax.optimization_barrier((output_low, grad_attended))
    output_part = lax.psum_scatter(output_low, "fsdp", scatter_dimension=0, tiled=True)
    grad_pre, query_gain_part, key_gain_part = attend_back(
        pre, tables, gains, attended, grad_attended, rows, heads, kv_heads
    )
    qkv_low = mm(normed_rows, grad_pre, ((0,), (0,))).astype(BF16)
    qkv_grad = ring_scatter(qkv_low.reshape(nodes, -1, qkv_low.shape[1]))
    qkv_grad = qkv_grad.reshape(query_weight.shape[0], -1)
    grad_normed = mm(grad_pre, qkv_full, ((1,), (1,))).reshape(rows, tp_size, local_length, model_width)
    grad_one = scatter_tp([grad_normed[:, j] for j in range(tp_size)])
    attention_gain_part = jnp.sum(grad_one * normed_one, axis=(0, 1))
    input_grad = grad_middle + norm_backward(grad_one, attention_gain, normed_one, inverse_one)

    moved = []
    for kind in range(3):
        for j in range(1, tp_size):
            far = jnp.stack([far_grads[e][j - 1][kind] for e in range(local_experts)])
            moved.append(lax.ppermute(far, "tp", [(s, (s + j) % tp_size) for s in range(tp_size)]))
    moved, qkv_grad = lax.optimization_barrier((moved, qkv_grad))
    weight_grads = []
    for kind in range(3):
        total = jnp.stack([own_grads[e][kind] for e in range(local_experts)])
        for j in range(tp_size - 1):
            total = total + moved[kind * (tp_size - 1) + j].astype(F32)
        weight_grads.append(total)
    gate_grad, up_grad, down_grad = weight_grads
    query_width, key_width = query_weight.shape[1], key_weight.shape[1]
    query_grad = qkv_grad[:, :query_width]
    key_grad = qkv_grad[:, query_width : query_width + key_width]
    value_grad = qkv_grad[:, query_width + key_width :]

    layer_output = (middle + expert_part.reshape(middle.shape).astype(F32)).astype(BF16)
    output_grad = output_part.astype(F32)

    kept = [
        value.reshape(nodes, tp_size, -1)
        for value in (
            router_part,
            attention_gain_part,
            expert_gain_part,
            query_gain_part,
            key_gain_part,
        )
    ]
    sizes = [value.shape[2] for value in kept]
    shares = jnp.concatenate(kept, axis=2)
    shares = jnp.pad(shares, ((0, 0), (0, 0), (0, -shares.shape[2] % 128)))
    shares = lax.all_to_all(
        shares.reshape(nodes, tp_size, -1, 128), "fsdp", split_axis=0, concat_axis=0, tiled=True
    )
    shares = jnp.sum(shares, axis=0)
    mine = jnp.zeros(shares.shape[1:], F32)
    for j in range(tp_size):
        share = lax.dynamic_index_in_dim(shares, (part + j) % tp_size, 0, keepdims=False)
        if j > 0:
            share = lax.ppermute(share, "tp", [(s, (s + j) % tp_size) for s in range(tp_size)])
        mine = mine + share
    mine = mine.reshape(-1)
    small = []
    at = 0
    for size in sizes:
        small.append(mine[at : at + size])
        at += size
    router_grad = small[0].reshape(-1, expert_count)
    attention_gain_grad, expert_gain_grad, query_gain_grad, key_gain_grad = small[1:]
    return (
        layer_output,
        input_grad,
        attention_gain_grad,
        query_gain_grad,
        key_gain_grad,
        query_grad,
        key_grad,
        value_grad,
        output_grad,
        router_grad,
        expert_gain_grad,
        gate_grad,
        up_grad,
        down_grad,
    )


def solution(mesh):
    return jax.shard_map(
        layer,
        mesh=mesh,
        in_specs=(
            P("fsdp", "tp", None),
            P(),
            P(),
            P(),
            P("fsdp", "tp"),
            P("fsdp", "tp"),
            P("fsdp", "tp"),
            P("fsdp", "tp"),
            P("fsdp", None),
            P(),
            P("fsdp", None, "tp"),
            P("fsdp", None, "tp"),
            P("fsdp", "tp", None),
            P("fsdp", None, None),
            P("fsdp", None),
            P("fsdp", "tp", None),
        ),
        out_specs=(
            P("fsdp", "tp", None),
            P("fsdp", "tp", None),
            P(("fsdp", "tp")),
            P(("fsdp", "tp")),
            P(("fsdp", "tp")),
            P("fsdp", "tp"),
            P("fsdp", "tp"),
            P("fsdp", "tp"),
            P("fsdp", "tp"),
            P(("fsdp", "tp"), None),
            P(("fsdp", "tp")),
            P("fsdp", None, "tp"),
            P("fsdp", None, "tp"),
            P("fsdp", "tp", None),
        ),
        check_vma=False,
    )
```

```python
import functools
import math

import jax
import jax.numpy as jnp
from jax import lax
from jax.experimental import pallas as pl
from jax.experimental.pallas import tpu as pltpu
from jax.sharding import PartitionSpec as P


EPSILON = 1e-06
ROPE_BASE = 1000000.0
NEGATIVE = -1e30
F32 = jnp.float32
BF16 = jnp.bfloat16


def inverse_rms(values):
    return lax.rsqrt(jnp.mean(values * values, axis=-1, keepdims=True) + EPSILON)


def norm_backward(grad_scaled, gain, normed, inverse):
    grad_normed = grad_scaled * gain
    return inverse * (grad_normed - normed * jnp.mean(grad_normed * normed, axis=-1, keepdims=True))


def mm(a, b, dims=((1,), (0,))):
    return lax.dot_general(a, b, (dims, ((), ())), preferred_element_type=F32)


def fetch_next(values, step):
    size = lax.axis_size("tp")
    return lax.ppermute(values, "tp", [(s, (s - step) % size) for s in range(size)])


def gather_tp(values, axis):
    size = lax.axis_size("tp")
    return jnp.concatenate([values] + [fetch_next(values, j) for j in range(1, size)], axis=axis)


def scatter_tp(pieces):
    size = lax.axis_size("tp")
    total = pieces[0].astype(F32)
    for j in range(1, size):
        moved = lax.ppermute(
            pieces[j].astype(BF16), "tp", [(s, (s + j) % size) for s in range(size)]
        )
        total = total + moved.astype(F32)
    return total


def chip_ring(nodes):
    chips = nodes // 2
    order = list(range(0, chips, 2)) + list(range(1, chips, 2))[::-1]
    links = [(order[i] * 2 + c, order[(i + 1) % chips] * 2 + c) for i in range(chips) for c in (0, 1)]
    swap = [(i, i ^ 1) for i in range(nodes)]
    return order, links, [(b, a) for a, b in links], swap


def ring_fits(nodes):
    return nodes % 4 == 0 and 8 <= nodes <= 16


def node_at(order, shift, core):
    place = jnp.asarray([order.index(i) for i in range(len(order))], jnp.int32)
    mine = place[lax.axis_index("fsdp") // 2]
    return jnp.asarray(order, jnp.int32)[(mine + shift) % len(order)] * 2 + core


def ring_gather(block, between):
    nodes = lax.axis_size("fsdp")
    if not ring_fits(nodes):
        for work in between:
            work(())
        return lax.all_gather(block, "fsdp", axis=0)
    order, up, down, swap = chip_ring(nodes)
    core = lax.axis_index("fsdp") % 2
    whole = jnp.zeros((nodes,) + block.shape, block.dtype)

    def keep(whole, piece, shift):
        other = lax.ppermute(piece, "fsdp", swap)
        for values, at in ((piece, core), (other, 1 - core)):
            whole = lax.dynamic_update_index_in_dim(whole, values, node_at(order, shift, at), 0)
        return whole

    whole = keep(whole, block, 0)
    ahead = behind = block
    for step in range(1, len(order) // 2 + 1):
        behind = lax.ppermute(behind, "fsdp", up)
        if step < (len(order) + 1) // 2:
            ahead = lax.ppermute(ahead, "fsdp", down)
        if step <= len(between):
            behind, ahead = between[step - 1]((behind, ahead))
        whole = keep(whole, behind, -step)
        if step < (len(order) + 1) // 2:
            whole = keep(whole, ahead, step)
    return whole


def ring_scatter(blocks):
    nodes = lax.axis_size("fsdp")
    if not ring_fits(nodes):
        return lax.psum_scatter(blocks, "fsdp", scatter_dimension=0, tiled=False).astype(F32)
    order, up, down, swap = chip_ring(nodes)
    core = lax.axis_index("fsdp") % 2

    def chip_sum(shift):
        mine = lax.dynamic_index_in_dim(blocks, node_at(order, shift, core), 0, keepdims=False)
        away = lax.dynamic_index_in_dim(blocks, node_at(order, shift, 1 - core), 0, keepdims=False)
        return mine.astype(F32) + lax.ppermute(away, "fsdp", swap).astype(F32)

    far = len(order) // 2
    rising = chip_sum(far).astype(BF16)
    falling = chip_sum(far + 1).astype(BF16)
    for step in range(far - 1, -1, -1):
        rising = lax.ppermute(rising, "fsdp", up).astype(F32)
        if step > 0:
            rising = (rising + chip_sum(step)).astype(BF16)
        if step < far - 1:
            falling = lax.ppermute(falling, "fsdp", down).astype(F32)
            if step > 0:
                falling = (falling + chip_sum(-step)).astype(BF16)
    return rising + falling + chip_sum(0)


def turn(values, cosine, sine):
    return values * cosine + pltpu.roll(values, values.shape[-1] // 2, 1) * sine


def turn_back(values, cosine, sine):
    return values * cosine - pltpu.roll(values, values.shape[-1] // 2, 1) * sine


def normed_turned(pre, gain, cosine, sine):
    inverse = inverse_rms(pre)
    normed = pre * inverse
    return inverse, normed, turn(normed * gain, cosine, sine).astype(BF16)


def weights_of(query_rot, key_rot, bias):
    factor = 1.0 / math.sqrt(query_rot.shape[-1])
    scores = mm(query_rot, key_rot, ((1,), (1,))) * factor + bias
    powers = jnp.exp(scores - jnp.max(scores, axis=-1, keepdims=True))
    return powers * (1.0 / jnp.sum(powers, axis=-1, keepdims=True))


def attend_kernel(q_ref, k_ref, v_ref, cos_ref, sin_ref, bias_ref, qg_ref, kg_ref, out_ref, key_rot):
    cosine, sine = cos_ref[...], sin_ref[...]

    @pl.when(pl.program_id(2) == 0)
    def _():
        key_rot[...] = normed_turned(k_ref[...], kg_ref[...], cosine, sine)[2]

    query_rot = normed_turned(q_ref[...], qg_ref[...], cosine, sine)[2]
    weights = weights_of(query_rot, key_rot[...], bias_ref[...])
    out_ref[...] = mm(weights.astype(BF16), v_ref[...].astype(BF16)).astype(BF16)


def attend_back_kernel(
    q_ref, k_ref, v_ref, cos_ref, sin_ref, bias_ref, qg_ref, kg_ref, att_ref, go_ref,
    grad_ref, qgain_ref, kgain_ref, key_rot, key_normed, key_inverse, grad_key, grad_value,
):
    row, kv, step = pl.program_id(0), pl.program_id(1), pl.program_id(2)
    group_size = pl.num_programs(2) - 2
    cosine, sine = cos_ref[...], sin_ref[...]
    factor = 1.0 / math.sqrt(q_ref.shape[-1])

    @pl.when((row == 0) & (kv == 0) & (step == 0))
    def _():
        qgain_ref[...] = jnp.zeros_like(qgain_ref)
        kgain_ref[...] = jnp.zeros_like(kgain_ref)

    @pl.when(step == 0)
    def _():
        inverse, normed, rotated = normed_turned(k_ref[...], kg_ref[...], cosine, sine)
        key_rot[...] = rotated
        key_normed[...] = normed
        key_inverse[...] = jnp.broadcast_to(inverse, key_inverse.shape)
        grad_key[...] = jnp.zeros_like(grad_key)
        grad_value[...] = jnp.zeros_like(grad_value)

    @pl.when(step < group_size)
    def _():
        inverse, normed, query_rot = normed_turned(q_ref[...], qg_ref[...], cosine, sine)
        weights = weights_of(query_rot, key_rot[...], bias_ref[...])
        grad_out = go_ref[...]
        grad_value[...] += mm(weights.astype(BF16), grad_out, ((0,), (0,)))
        grad_weights = mm(grad_out, v_ref[...].astype(BF16), ((1,), (1,)))
        delta = jnp.sum(att_ref[...].astype(F32) * grad_out.astype(F32), axis=-1, keepdims=True)
        grad_scores = (weights * (grad_weights - delta) * factor).astype(BF16)
        grad_query = turn_back(mm(grad_scores, key_rot[...]), cosine, sine)
        grad_key[...] += mm(grad_scores, query_rot, ((0,), (0,)))
        qgain_ref[...] += jnp.sum(grad_query * normed, axis=0, keepdims=True)
        grad_ref[...] = norm_backward(grad_query, qg_ref[...], normed, inverse).astype(BF16)

    @pl.when(step == group_size)
    def _():
        grad = turn_back(grad_key[...], cosine, sine)
        normed = key_normed[...]
        kgain_ref[...] += jnp.sum(grad * normed, axis=0, keepdims=True)
        grad_ref[...] = norm_backward(
            grad, kg_ref[...], normed, key_inverse[...][:, :1]
        ).astype(BF16)

    @pl.when(step == group_size + 1)
    def _():
        grad_ref[...] = grad_value[...].astype(BF16)


def attention_specs(length, head_size, heads, kv_heads):
    group_size = heads // kv_heads

    def head(r, kv, g):
        return (r, kv * group_size + jnp.minimum(g, group_size - 1))

    block = (length, head_size)
    full = pl.BlockSpec((1, head_size), lambda r, kv, g: (0, 0))
    return head, [
        pl.BlockSpec(block, head),
        pl.BlockSpec(block, lambda r, kv, g: (r, heads + kv)),
        pl.BlockSpec(block, lambda r, kv, g: (r, heads + kv_heads + kv)),
        pl.BlockSpec(block, lambda r, kv, g: (r, 0)),
        pl.BlockSpec(block, lambda r, kv, g: (r, 0)),
        pl.BlockSpec((None, length, length), lambda r, kv, g: (r, 0, 0)),
        full,
        full,
    ]


def attend(pre, tables, gains, rows, heads, kv_heads):
    length, head_size = pre.shape[0] // rows, gains[0].shape[1]
    head, specs = attention_specs(length, head_size, heads, kv_heads)
    cost = rows * heads * length * length
    return pl.pallas_call(
        attend_kernel,
        grid=(rows, kv_heads, heads // kv_heads),
        in_specs=specs,
        out_specs=pl.BlockSpec((length, head_size), head),
        out_shape=jax.ShapeDtypeStruct((pre.shape[0], heads * head_size), BF16),
        scratch_shapes=[pltpu.VMEM((length, head_size), BF16)],
        cost_estimate=pl.CostEstimate(
            flops=4 * cost * head_size, bytes_accessed=6 * pre.size, transcendentals=cost
        ),
        name="attend",
    )(pre, pre, pre, *tables, *gains)


def attend_back(pre, tables, gains, attended, grad_attended, rows, heads, kv_heads):
    length, head_size = pre.shape[0] // rows, gains[0].shape[1]
    group_size = heads // kv_heads
    head, specs = attention_specs(length, head_size, heads, kv_heads)

    def target(r, kv, g):
        own = kv * group_size + g
        return (r, jnp.where(g < group_size, own, heads + kv + jnp.where(g > group_size, kv_heads, 0)))

    block = pl.BlockSpec((length, head_size), head)
    full = pl.BlockSpec((1, head_size), lambda r, kv, g: (0, 0))
    gain = jax.ShapeDtypeStruct((1, head_size), F32)
    cost = rows * heads * length * length
    wide = pltpu.VMEM((length, head_size), F32)
    return pl.pallas_call(
        attend_back_kernel,
        grid=(rows, kv_heads, group_size + 2),
        in_specs=specs + [block, block],
        out_specs=[pl.BlockSpec((length, head_size), target), full, full],
        out_shape=[jax.ShapeDtypeStruct(pre.shape, BF16), gain, gain],
        scratch_shapes=[pltpu.VMEM((length, head_size), BF16), wide, wide, wide, wide],
        cost_estimate=pl.CostEstimate(
            flops=10 * cost * head_size, bytes_accessed=10 * pre.size, transcendentals=cost
        ),
        name="attend_back",
    )(pre, pre, pre, *tables, *gains, attended, grad_attended)


TILE = 256
PACK = 16
GRANT = 60 * 1024 * 1024
HELD = 20 * 1024 * 1024


def pick_kernel(tiles, first, last, places_ref, *refs):
    e, j = pl.program_id(1), pl.program_id(2)
    third = len(refs) // 3
    sources, outs, totals = refs[:third], refs[third : 2 * third], refs[2 * third :]

    @pl.when(j < tiles[e])
    def _():
        for total in totals:
            total[...] = jnp.zeros_like(total)
        at = e * pl.num_programs(2) + j
        wanted = j * TILE + lax.broadcasted_iota(jnp.int32, (TILE, places_ref.shape[2]), 0)

        def add(g, carry):
            hits = jnp.where(places_ref[g] == wanted, 1.0, 0.0).astype(BF16)
            for source, total in zip(sources, totals):
                total[...] += mm(hits, source[g])
            return carry

        lax.fori_loop(first[at], last[at] + 1, add, 0)
        for out, total in zip(outs, totals):
            out[...] = total[...].astype(BF16)

    @pl.when(j >= tiles[e])
    def _():
        for out in outs:
            out[...] = jnp.zeros_like(out)


def pick(plan, source, width):
    experts, nodes, _, tokens = plan["places"].shape
    count = plan["tile_count"]
    cuts = 1
    while 2 * nodes * tokens * (width // cuts) > HELD and width % (256 * cuts) == 0:
        cuts *= 2
    part = width // cuts
    more = source.shape[2] - width
    out_specs = [pl.BlockSpec((None, TILE, part), lambda c, e, j, *_: (e, j, c))]
    in_specs = [
        pl.BlockSpec((None, nodes, 1, tokens), lambda c, e, j, *_: (e, 0, 0, 0)),
        pl.BlockSpec(
            (nodes, tokens, part), lambda c, e, j, *_: (0, 0, c), pipeline_mode=pl.Buffered(1)
        ),
    ]
    widths = [width]
    scratch = [pltpu.VMEM((TILE, part), F32)]
    if more:
        out_specs.append(pl.BlockSpec((None, TILE, more), lambda c, e, j, *_: (e, j, 0)))
        in_specs.append(
            pl.BlockSpec(
                (nodes, tokens, more),
                lambda c, e, j, *_: (0, 0, width // more),
                pipeline_mode=pl.Buffered(1),
            )
        )
        widths.append(more)
        scratch.append(pltpu.VMEM((TILE, more), F32))
    return pl.pallas_call(
        pick_kernel,
        grid_spec=pltpu.PrefetchScalarGridSpec(
            num_scalar_prefetch=3,
            grid=(cuts, experts, count),
            in_specs=in_specs,
            out_specs=out_specs,
            scratch_shapes=scratch,
        ),
        out_shape=[jax.ShapeDtypeStruct((experts, count * TILE, w), BF16) for w in widths],
        compiler_params=pltpu.CompilerParams(vmem_limit_bytes=GRANT),
        cost_estimate=pl.CostEstimate(
            flops=6 * experts * count * TILE * tokens * width,
            bytes_accessed=2 * nodes * tokens * width + 2 * experts * count * TILE * width,
            transcendentals=0,
        ),
        name="pick",
    )(
        plan["tiles"], plan["first"], plan["last"], plan["places"], *([source] * len(widths))
    )


def weight_kernel(tiles, left_ref, right_ref, own_ref, far_ref, total, *, axis, piece, group):
    e, j = pl.program_id(0), pl.program_id(1)

    @pl.when(j == 0)
    def _():
        total[...] = jnp.zeros_like(total)

    @pl.when(j * group < tiles[e])
    def _():
        total[...] += mm(left_ref[...], right_ref[...], ((0,), (0,)))

    @pl.when(j == pl.num_programs(1) - 1)
    def _():
        if axis == 0:
            own_ref[...] = total[:piece, :]
            far_ref[...] = total[piece:, :].astype(BF16)
        else:
            own_ref[...] = total[:, :piece]
            far_ref[...] = total[:, piece:].astype(BF16)


def weight_grad(plan, left, right, axis, piece):
    experts, height, deep = left.shape
    wide = right.shape[2]
    group = 2 if plan["tile_count"] % 2 == 0 else 1
    size = group * TILE

    def block(rows, columns):
        return pl.BlockSpec((None, rows, columns), lambda e, j, *_: (e, 0, 0))

    own = (piece, wide) if axis == 0 else (deep, piece)
    far = (deep - piece, wide) if axis == 0 else (deep, wide - piece)

    def rows_at(e, j, tiles):
        used = (tiles[e] + group - 1) // group
        return (e, jnp.minimum(j, jnp.maximum(used - 1, 0)), 0)

    return pl.pallas_call(
        functools.partial(weight_kernel, axis=axis, piece=piece, group=group),
        grid_spec=pltpu.PrefetchScalarGridSpec(
            num_scalar_prefetch=1,
            grid=(experts, height // size),
            in_specs=[
                pl.BlockSpec((None, size, deep), rows_at),
                pl.BlockSpec((None, size, wide), rows_at),
            ],
            out_specs=[block(*own), block(*far)],
            scratch_shapes=[pltpu.VMEM((deep, wide), F32)],
        ),
        out_shape=[
            jax.ShapeDtypeStruct((experts,) + own, F32),
            jax.ShapeDtypeStruct((experts,) + far, BF16),
        ],
        compiler_params=pltpu.CompilerParams(vmem_limit_bytes=GRANT),
        cost_estimate=pl.CostEstimate(
            flops=experts * height * deep * wide,
            bytes_accessed=experts * (height * (deep + wide) + 6 * deep * wide),
            transcendentals=0,
        ),
        name="weight_grad",
    )(plan["tiles"], left, right)


def expert_kernel(
    tiles, base, arrived_ref, extra_ref, cots_ref, gate_ref, up_ref, down_ref,
    weighed_ref, grad_gate_ref, grad_up_ref, produced_ref, back_ref, column_ref, *, expert_count,
):
    e, j = pl.program_id(0), pl.program_id(1)

    @pl.when(j < tiles[e])
    def _():
        lane = lax.broadcasted_iota(jnp.int32, extra_ref.shape, 1)
        own = base[0] + e
        gates = jnp.where(
            (lane == own) | (lane == own + expert_count), extra_ref[...].astype(F32), 0.0
        )
        gate_here = jnp.sum(gates, axis=-1, keepdims=True)
        gate_pre = mm(arrived_ref[...], gate_ref[...])
        up_pre = mm(arrived_ref[...], up_ref[...])
        grad_plain = mm(cots_ref[...], down_ref[...], ((1,), (1,)))
        sigmoid_gate = 1.0 / (1.0 + jnp.exp(-gate_pre))
        activated = gate_pre * sigmoid_gate
        hidden = activated * up_pre
        column = jnp.sum(hidden * grad_plain, axis=-1, keepdims=True)
        high = column.astype(BF16).astype(F32)
        spot = lax.broadcasted_iota(jnp.int32, column_ref.shape, 1)
        column_ref[...] = jnp.where(
            spot == 2 * e, high, jnp.where(spot == 2 * e + 1, column - high, 0.0)
        ).astype(BF16)
        weighed = (hidden * gate_here).astype(BF16)
        weighed_ref[...] = weighed
        grad_hidden = grad_plain * gate_here
        grad_gate = (
            grad_hidden * up_pre * sigmoid_gate * (1.0 + gate_pre * (1.0 - sigmoid_gate))
        ).astype(BF16)
        grad_up = (grad_hidden * activated).astype(BF16)
        grad_gate_ref[...] = grad_gate
        grad_up_ref[...] = grad_up
        produced_ref[...] = mm(weighed, down_ref[...]).astype(BF16)
        back_ref[...] = (
            mm(grad_gate, gate_ref[...], ((1,), (1,))) + mm(grad_up, up_ref[...], ((1,), (1,)))
        ).astype(BF16)

    @pl.when(j >= tiles[e])
    def _():
        for ref in (weighed_ref, grad_gate_ref, grad_up_ref, produced_ref, back_ref, column_ref):
            ref[...] = jnp.zeros_like(ref)


def run_experts(plan, base, arrived, extra, cots, gate, up, down, expert_count):
    experts, height, width = arrived.shape
    hidden = gate.shape[2]
    count = plan["tile_count"]

    def tile(size):
        return pl.BlockSpec((None, TILE, size), lambda e, j, *_: (e, j, 0))

    def whole(shape):
        return pl.BlockSpec((None,) + shape, lambda e, j, *_: (e, 0, 0))

    def out(size):
        return jax.ShapeDtypeStruct((experts, height, size), BF16)

    return pl.pallas_call(
        functools.partial(expert_kernel, expert_count=expert_count),
        grid_spec=pltpu.PrefetchScalarGridSpec(
            num_scalar_prefetch=2,
            grid=(experts, count),
            in_specs=[
                tile(width), tile(extra.shape[2]), tile(width),
                whole((width, hidden)), whole((width, hidden)), whole((hidden, width)),
            ],
            out_specs=[tile(hidden)] * 3 + [tile(width)] * 2 + [tile(128)],
        ),
        out_shape=[out(hidden)] * 3 + [out(width)] * 2 + [out(128)],
        compiler_params=pltpu.CompilerParams(vmem_limit_bytes=GRANT),
        cost_estimate=pl.CostEstimate(
            flops=6 * experts * height * width * hidden,
            bytes_accessed=2 * experts * (4 * height * width + 3 * height * hidden),
            transcendentals=experts * height * hidden // 2,
        ),
        name="run_experts",
    )(plan["tiles"], base, arrived, extra, cots, gate, up, down)


def spread_kernel(starts, places_ref, *refs):
    g = pl.program_id(0)
    half = len(refs) // 2
    experts, nodes = places_ref.shape[0], pl.num_programs(0)
    window = refs[-1]
    size = window.shape[0]
    totals = [None] * half
    for e in range(experts):
        start = pl.multiple_of(starts[e * nodes + g], PACK)
        wanted = start + lax.broadcasted_iota(jnp.int32, (size, places_ref.shape[2]), 0)
        hits = jnp.where(places_ref[e] == wanted, 1.0, 0.0).astype(BF16)
        for i in range(half):
            part = mm(hits, refs[i][e, pl.ds(start, size), :], ((0,), (0,)))
            totals[i] = part if totals[i] is None else totals[i] + part
    for i in range(half):
        refs[half + i][...] = totals[i].astype(BF16)


def spread(plan, sources):
    experts, nodes, _, tokens = plan["places"].shape
    window = plan["window"]
    return pl.pallas_call(
        spread_kernel,
        grid_spec=pltpu.PrefetchScalarGridSpec(
            num_scalar_prefetch=1,
            grid=(nodes,),
            in_specs=[pl.BlockSpec((experts, None, 1, tokens), lambda g, *_: (0, g, 0, 0))]
            + [
                pl.BlockSpec(source.shape, lambda g, *_: (0, 0, 0), pipeline_mode=pl.Buffered(1))
                for source in sources
            ],
            out_specs=[
                pl.BlockSpec((None, tokens, source.shape[2]), lambda g, *_: (g, 0, 0))
                for source in sources
            ],
            scratch_shapes=[pltpu.VMEM((window, 128), BF16)],
        ),
        out_shape=[
            jax.ShapeDtypeStruct((nodes, tokens, source.shape[2]), BF16) for source in sources
        ],
        compiler_params=pltpu.CompilerParams(vmem_limit_bytes=GRANT),
        cost_estimate=pl.CostEstimate(
            flops=2 * experts * nodes * tokens * window * sum(s.shape[2] for s in sources),
            bytes_accessed=sum(4 * s.size for s in sources),
            transcendentals=0,
        ),
        name="spread",
    )(plan["starts"], plan["places"], *sources)


def plan_places(member, slot, places):
    nodes, _, _ = member.shape
    counts = jnp.sum(member.astype(jnp.int32), axis=2)
    earlier = jnp.arange(nodes)[:, None] > jnp.arange(nodes)[None, :]
    offset = jnp.sum(jnp.where(earlier[:, :, None], counts[None], 0), axis=1)
    totals = jnp.sum(counts, axis=0)
    count = -(-(nodes * places) // TILE)
    edges = jnp.arange(count, dtype=jnp.int32) * TILE
    ends = offset + counts
    first = jnp.sum((ends[:, :, None] <= edges).astype(jnp.int32), axis=0)
    last = jnp.sum((offset[:, :, None] < edges + TILE).astype(jnp.int32), axis=0) - 1
    window = -(-places // PACK) * PACK + PACK
    window = min(window, count * TILE)
    starts = jnp.minimum(offset // PACK * PACK, count * TILE - window)
    packed = jnp.where(member, offset[:, :, None] + slot, -1)
    return {
        "places": jnp.moveaxis(packed, 1, 0)[:, :, None, :],
        "tiles": (totals + TILE - 1) // TILE,
        "first": jnp.minimum(first, nodes - 1).reshape(-1),
        "last": jnp.minimum(last, nodes - 1).reshape(-1),
        "starts": starts.T.reshape(-1),
        "tile_count": count,
        "window": window,
    }


def layer(
    layer_input,
    attention_gain,
    query_gain,
    key_gain,
    query_weight,
    key_weight,
    value_weight,
    output_weight,
    router_weight,
    expert_gain,
    gate_weight,
    up_weight,
    down_weight,
    routes,
    segments,
    cotangent,
):
    rows, local_length, model_width = layer_input.shape
    length = segments.shape[1]
    head_size = query_gain.shape[0]
    expert_count = router_weight.shape[1]
    local_experts, _, half_hidden = gate_weight.shape
    top_count = routes.shape[2]
    nodes = lax.axis_size("fsdp")
    tp_size = lax.axis_size("tp")
    node = lax.axis_index("fsdp")
    part = lax.axis_index("tp")
    heads = query_weight.shape[1] // head_size
    kv_heads = key_weight.shape[1] // head_size
    capacity = max(2, rows * length * top_count * 5 // (4 * expert_count))
    tokens = rows * local_length
    places = min(capacity, tokens)
    every = tp_size * tokens

    qkv_full = lax.all_gather(
        jnp.concatenate([query_weight, key_weight, value_weight], axis=1), "fsdp", axis=0, tiled=True
    )
    input_wide = layer_input.astype(F32)
    inverse_one = inverse_rms(input_wide)
    normed_one = input_wide * inverse_one
    normed_low = (normed_one * attention_gain).astype(BF16)
    normed_rows = gather_tp(normed_low, 1).reshape(every, model_width)
    output_full = lax.all_gather(output_weight, "fsdp", axis=0, tiled=True)
    router_full = lax.all_gather(router_weight, "fsdp", axis=0, tiled=True)

    places_in = jnp.concatenate(
        [
            ((part + j) % tp_size) * local_length + jnp.arange(local_length, dtype=jnp.int32)
            for j in range(tp_size)
        ]
    )
    doubled = jnp.concatenate([segments, segments], axis=1)
    ids = lax.dynamic_slice_in_dim(doubled, part * local_length, length, axis=1)
    starts = jnp.sum((segments[:, None, :] < ids[:, :, None]).astype(jnp.int32), axis=2)
    half_size = head_size // 2
    frequency = jnp.exp(jnp.arange(half_size, dtype=F32) * (-2.0 * math.log(ROPE_BASE) / head_size))
    angles = (places_in[None, :] - starts).astype(F32)[:, :, None] * frequency
    cosine, sine = jnp.cos(angles), jnp.sin(angles)
    cosine_table = jnp.concatenate([cosine, cosine], axis=-1).reshape(every, head_size)
    sine_table = jnp.concatenate([-sine, sine], axis=-1).reshape(every, head_size)
    allowed = (ids[:, :, None] == ids[:, None, :]) & (places_in[None, :] <= places_in[:, None])[None]
    tables = (cosine_table, sine_table, jnp.where(allowed, 0.0, NEGATIVE).astype(F32))
    gains = (query_gain.reshape(1, head_size), key_gain.reshape(1, head_size))

    gate_weight, up_weight, down_weight, normed_rows = lax.optimization_barrier(
        (gate_weight, up_weight, down_weight, normed_rows)
    )
    gate_full = gather_tp(gate_weight, 2)
    up_full = gather_tp(up_weight, 2)

    own_routes = lax.dynamic_slice_in_dim(routes, part * local_length, local_length, axis=1)
    own_routes = own_routes.reshape(tokens, top_count)
    all_routes = lax.all_gather(own_routes, "fsdp", axis=0).reshape(nodes, tokens, top_count)
    own_experts = node * local_experts + jnp.arange(local_experts, dtype=jnp.int32)
    member = jnp.any(all_routes[:, None, :, :] == own_experts[None, :, None, None], axis=-1)
    before = jnp.arange(tokens)[:, None] < jnp.arange(tokens)[None, :]
    slot = jnp.einsum(
        "get,tu->geu", member.astype(BF16), before.astype(BF16), preferred_element_type=F32
    ).astype(jnp.int32)
    plan = plan_places(member, slot, places)
    base = (node * local_experts).reshape(1).astype(jnp.int32)

    normed_rows, router_full, all_routes = lax.optimization_barrier(
        (normed_rows, router_full, all_routes)
    )
    pre = mm(normed_rows, qkv_full)
    cot_low = cotangent.reshape(tokens, model_width)
    cot_low, pre = lax.optimization_barrier((cot_low, pre))
    attended = attend(pre, tables, gains, rows, heads, kv_heads)
    made = {}

    def project(moving):
        held, moving = lax.optimization_barrier((attended, moving))
        projected = mm(held, output_full, ((1,), (1,)))
        projected = projected.reshape(rows, tp_size, local_length, model_width)
        made["middle"] = input_wide + scatter_tp([projected[:, j] for j in range(tp_size)])
        return moving

    def settle(moving):
        made["middle"], moving = lax.optimization_barrier((made["middle"], moving))
        return moving

    cot_all = ring_gather(cot_low, (project, settle))
    middle, down_weight = lax.optimization_barrier((made["middle"], down_weight))
    down_full = gather_tp(down_weight, 1)
    inverse_two = inverse_rms(middle)
    normed_two = middle * inverse_two
    expert_low = (normed_two * expert_gain).astype(BF16).reshape(tokens, model_width)

    logits = mm(expert_low, router_full)
    chosen = jnp.any(
        own_routes[:, :, None] == jnp.arange(expert_count, dtype=jnp.int32), axis=1
    )
    top = jnp.max(jnp.where(chosen, logits, NEGATIVE), axis=-1, keepdims=True)
    powers = jnp.where(chosen, jnp.exp(jnp.minimum(logits - top, 0.0)), 0.0)
    gates = powers / jnp.sum(powers, axis=-1, keepdims=True)
    high = lax.reduce_precision(gates, 8, 7)
    filler = jnp.zeros((tokens, -2 * expert_count % 128), BF16)
    sent = jnp.concatenate(
        [expert_low, high.astype(BF16), (gates - high).astype(BF16), filler], axis=1
    )
    rows_all = lax.all_gather(sent, "fsdp", axis=0)

    arrived, extra = pick(plan, rows_all, model_width)
    cots = pick(plan, cot_all, model_width)[0]
    weighed, grad_gate_pre, grad_up_pre, produced, back, columns = run_experts(
        plan, base, arrived, extra, cots, gate_full, up_full, down_full, expert_count
    )
    out_total = spread(plan, [produced])[0]
    out_total, back = lax.optimization_barrier((out_total, back))
    grad_total, columns = spread(plan, [back, columns])
    own_grads, far_grads = zip(
        weight_grad(plan, arrived, grad_gate_pre, 1, half_hidden),
        weight_grad(plan, arrived, grad_up_pre, 1, half_hidden),
        weight_grad(plan, weighed, cots, 0, half_hidden),
    )

    pairs = columns[:, :, : 2 * local_experts].astype(F32).reshape(nodes, tokens, local_experts, 2)
    column = jnp.sum(pairs, axis=-1)
    grad_gate = lax.all_to_all(column, "fsdp", split_axis=0, concat_axis=0, tiled=True)
    grad_gate = jnp.moveaxis(grad_gate, 0, 1).reshape(tokens, expert_count)

    moved = []
    for kind in range(3):
        axis = 2 if kind < 2 else 1
        moved.append(
            [
                lax.ppermute(
                    lax.slice_in_dim(
                        far_grads[kind], (j - 1) * half_hidden, j * half_hidden, axis=axis
                    ),
                    "tp",
                    [(s, (s + j) % tp_size) for s in range(tp_size)],
                )
                for j in range(1, tp_size)
            ]
        )
    grad_rows = ring_scatter(grad_total)
    expert_part = lax.psum_scatter(out_total, "fsdp", scatter_dimension=0, tiled=True)
    grad_logits = (
        gates * (grad_gate - jnp.sum(gates * grad_gate, axis=-1, keepdims=True))
    ).astype(BF16)
    router_part = mm(expert_low, grad_logits, ((0,), (0,)))
    grad_two = grad_rows.reshape(tokens, model_width).astype(F32) + mm(
        grad_logits, router_full, ((1,), (1,))
    )
    grad_two = grad_two.reshape(middle.shape)
    expert_gain_part = jnp.sum(grad_two * normed_two, axis=(0, 1))
    grad_middle = cotangent.astype(F32) + norm_backward(grad_two, expert_gain, normed_two, inverse_two)

    grad_low = gather_tp(grad_middle.astype(BF16), 1)
    grad_flat = grad_low.reshape(every, model_width)
    grad_attended = mm(grad_flat, output_full).astype(BF16)
    output_low = mm(grad_flat, attended, ((0,), (0,))).astype(BF16)
    output_low, grad_attended, expert_part = lax.optimization_barrier(
        (output_low, grad_attended, expert_part)
    )
    output_part = lax.psum_scatter(output_low, "fsdp", scatter_dimension=0, tiled=True)
    grad_pre, query_gain_part, key_gain_part = attend_back(
        pre, tables, gains, attended, grad_attended, rows, heads, kv_heads
    )
    qkv_low = mm(normed_rows, grad_pre, ((0,), (0,))).astype(BF16)
    qkv_grad = ring_scatter(qkv_low.reshape(nodes, -1, qkv_low.shape[1]))
    qkv_grad = qkv_grad.reshape(query_weight.shape[0], -1)
    grad_normed = mm(grad_pre, qkv_full, ((1,), (1,))).reshape(rows, tp_size, local_length, model_width)
    received = [
        lax.ppermute(
            grad_normed[:, j].astype(BF16), "tp", [(s, (s + j) % tp_size) for s in range(tp_size)]
        )
        for j in range(1, tp_size)
    ]

    moved, received, qkv_grad = lax.optimization_barrier((moved, received, qkv_grad))
    grad_one = grad_normed[:, 0]
    for value in received:
        grad_one = grad_one + value.astype(F32)
    attention_gain_part = jnp.sum(grad_one * normed_one, axis=(0, 1))
    input_grad = grad_middle + norm_backward(grad_one, attention_gain, normed_one, inverse_one)
    weight_grads = []
    for kind in range(3):
        total = own_grads[kind]
        for value in moved[kind]:
            total = total + value.astype(F32)
        weight_grads.append(total)
    gate_grad, up_grad, down_grad = weight_grads
    query_width, key_width = query_weight.shape[1], key_weight.shape[1]
    query_grad = qkv_grad[:, :query_width]
    key_grad = qkv_grad[:, query_width : query_width + key_width]
    value_grad = qkv_grad[:, query_width + key_width :]

    layer_output = (middle + expert_part.reshape(middle.shape).astype(F32)).astype(BF16)
    output_grad = output_part.astype(F32)

    kept = [
        value.reshape(nodes, tp_size, -1)
        for value in (
            router_part,
            attention_gain_part,
            expert_gain_part,
            query_gain_part,
            key_gain_part,
        )
    ]
    sizes = [value.shape[2] for value in kept]
    shares = jnp.concatenate(kept, axis=2)
    shares = jnp.pad(shares, ((0, 0), (0, 0), (0, -shares.shape[2] % 128)))
    shares = lax.all_to_all(
        shares.reshape(nodes, tp_size, -1, 128), "fsdp", split_axis=0, concat_axis=0, tiled=True
    )
    shares = jnp.sum(shares, axis=0)
    mine = jnp.zeros(shares.shape[1:], F32)
    for j in range(tp_size):
        share = lax.dynamic_index_in_dim(shares, (part + j) % tp_size, 0, keepdims=False)
        if j > 0:
            share = lax.ppermute(share, "tp", [(s, (s + j) % tp_size) for s in range(tp_size)])
        mine = mine + share
    mine = mine.reshape(-1)
    small = []
    at = 0
    for size in sizes:
        small.append(mine[at : at + size])
        at += size
    router_grad = small[0].reshape(-1, expert_count)
    attention_gain_grad, expert_gain_grad, query_gain_grad, key_gain_grad = small[1:]
    return (
        layer_output,
        input_grad,
        attention_gain_grad,
        query_gain_grad,
        key_gain_grad,
        query_grad,
        key_grad,
        value_grad,
        output_grad,
        router_grad,
        expert_gain_grad,
        gate_grad,
        up_grad,
        down_grad,
    )


def solution(mesh):
    return jax.shard_map(
        layer,
        mesh=mesh,
        in_specs=(
            P("fsdp", "tp", None),
            P(),
            P(),
            P(),
            P("fsdp", "tp"),
            P("fsdp", "tp"),
            P("fsdp", "tp"),
            P("fsdp", "tp"),
            P("fsdp", None),
            P(),
            P("fsdp", None, "tp"),
            P("fsdp", None, "tp"),
            P("fsdp", "tp", None),
            P("fsdp", None, None),
            P("fsdp", None),
            P("fsdp", "tp", None),
        ),
        out_specs=(
            P("fsdp", "tp", None),
            P("fsdp", "tp", None),
            P(("fsdp", "tp")),
            P(("fsdp", "tp")),
            P(("fsdp", "tp")),
            P("fsdp", "tp"),
            P("fsdp", "tp"),
            P("fsdp", "tp"),
            P("fsdp", "tp"),
            P(("fsdp", "tp"), None),
            P(("fsdp", "tp")),
            P("fsdp", None, "tp"),
            P("fsdp", None, "tp"),
            P("fsdp", "tp", None),
        ),
        check_vma=False,
    )
```

```python
import functools
import math

import jax
import jax.numpy as jnp
from jax import lax
from jax.experimental import pallas as pl
from jax.experimental.pallas import tpu as pltpu
from jax.sharding import PartitionSpec as P


EPSILON = 1e-06
ROPE_BASE = 1000000.0
NEGATIVE = -1e30
F32 = jnp.float32
BF16 = jnp.bfloat16


def inverse_rms(values):
    return lax.rsqrt(jnp.mean(values * values, axis=-1, keepdims=True) + EPSILON)


def norm_backward(grad_scaled, gain, normed, inverse):
    grad_normed = grad_scaled * gain
    return inverse * (grad_normed - normed * jnp.mean(grad_normed * normed, axis=-1, keepdims=True))


def mm(a, b, dims=((1,), (0,))):
    return lax.dot_general(a, b, (dims, ((), ())), preferred_element_type=F32)


def fetch_next(values, step):
    size = lax.axis_size("tp")
    return lax.ppermute(values, "tp", [(s, (s - step) % size) for s in range(size)])


def gather_tp(values, axis):
    size = lax.axis_size("tp")
    return jnp.concatenate([values] + [fetch_next(values, j) for j in range(1, size)], axis=axis)


def scatter_tp(pieces):
    size = lax.axis_size("tp")
    total = pieces[0].astype(F32)
    for j in range(1, size):
        moved = lax.ppermute(
            pieces[j].astype(BF16), "tp", [(s, (s + j) % size) for s in range(size)]
        )
        total = total + moved.astype(F32)
    return total


def chip_ring(nodes):
    chips = nodes // 2
    order = list(range(0, chips, 2)) + list(range(1, chips, 2))[::-1]
    links = [(order[i] * 2 + c, order[(i + 1) % chips] * 2 + c) for i in range(chips) for c in (0, 1)]
    swap = [(i, i ^ 1) for i in range(nodes)]
    return order, links, [(b, a) for a, b in links], swap


def ring_fits(nodes):
    return nodes % 4 == 0 and 8 <= nodes <= 16


def node_at(order, shift, core):
    place = jnp.asarray([order.index(i) for i in range(len(order))], jnp.int32)
    mine = place[lax.axis_index("fsdp") // 2]
    return jnp.asarray(order, jnp.int32)[(mine + shift) % len(order)] * 2 + core


def ring_gather(block, between):
    nodes = lax.axis_size("fsdp")
    if not ring_fits(nodes):
        for work in between:
            work(())
        return lax.all_gather(block, "fsdp", axis=0)
    order, up, down, swap = chip_ring(nodes)
    core = lax.axis_index("fsdp") % 2
    whole = jnp.zeros((nodes,) + block.shape, block.dtype)

    def keep(whole, piece, shift):
        other = lax.ppermute(piece, "fsdp", swap)
        for values, at in ((piece, core), (other, 1 - core)):
            whole = lax.dynamic_update_index_in_dim(whole, values, node_at(order, shift, at), 0)
        return whole

    whole = keep(whole, block, 0)
    ahead = behind = block
    for step in range(1, len(order) // 2 + 1):
        behind = lax.ppermute(behind, "fsdp", up)
        if step < (len(order) + 1) // 2:
            ahead = lax.ppermute(ahead, "fsdp", down)
        if step <= len(between):
            behind, ahead, *rest = between[step - 1](
                (behind, ahead, whole) if step == 1 else (behind, ahead)
            )
            whole = rest[0] if rest else whole
        whole = keep(whole, behind, -step)
        if step < (len(order) + 1) // 2:
            whole = keep(whole, ahead, step)
    return whole


def ring_scatter(blocks):
    nodes = lax.axis_size("fsdp")
    if not ring_fits(nodes):
        return lax.psum_scatter(blocks, "fsdp", scatter_dimension=0, tiled=False).astype(F32)
    order, up, down, swap = chip_ring(nodes)
    core = lax.axis_index("fsdp") % 2

    def chip_sum(shift):
        mine = lax.dynamic_index_in_dim(blocks, node_at(order, shift, core), 0, keepdims=False)
        away = lax.dynamic_index_in_dim(blocks, node_at(order, shift, 1 - core), 0, keepdims=False)
        return mine.astype(F32) + lax.ppermute(away, "fsdp", swap).astype(F32)

    far = len(order) // 2
    rising = chip_sum(far).astype(BF16)
    falling = chip_sum(far + 1).astype(BF16)
    for step in range(far - 1, -1, -1):
        rising = lax.ppermute(rising, "fsdp", up).astype(F32)
        if step > 0:
            rising = (rising + chip_sum(step)).astype(BF16)
        if step < far - 1:
            falling = lax.ppermute(falling, "fsdp", down).astype(F32)
            if step > 0:
                falling = (falling + chip_sum(-step)).astype(BF16)
    return rising + falling + chip_sum(0)


def turn(values, cosine, sine):
    return values * cosine + pltpu.roll(values, values.shape[-1] // 2, 1) * sine


def turn_back(values, cosine, sine):
    return values * cosine - pltpu.roll(values, values.shape[-1] // 2, 1) * sine


def normed_turned(pre, gain, cosine, sine):
    inverse = inverse_rms(pre)
    normed = pre * inverse
    return inverse, normed, turn(normed * gain, cosine, sine).astype(BF16)


def weights_of(query_rot, key_rot, bias):
    factor = 1.0 / math.sqrt(query_rot.shape[-1])
    scores = mm(query_rot, key_rot, ((1,), (1,))) * factor + bias
    powers = jnp.exp(scores - jnp.max(scores, axis=-1, keepdims=True))
    return powers * (1.0 / jnp.sum(powers, axis=-1, keepdims=True))


def attend_kernel(q_ref, k_ref, v_ref, cos_ref, sin_ref, bias_ref, qg_ref, kg_ref, out_ref, key_rot):
    cosine, sine = cos_ref[...], sin_ref[...]

    @pl.when(pl.program_id(2) == 0)
    def _():
        key_rot[...] = normed_turned(k_ref[...], kg_ref[...], cosine, sine)[2]

    query_rot = normed_turned(q_ref[...], qg_ref[...], cosine, sine)[2]
    weights = weights_of(query_rot, key_rot[...], bias_ref[...])
    out_ref[...] = mm(weights.astype(BF16), v_ref[...].astype(BF16)).astype(BF16)


def attend_back_kernel(
    q_ref, k_ref, v_ref, cos_ref, sin_ref, bias_ref, qg_ref, kg_ref, att_ref, go_ref,
    grad_ref, qgain_ref, kgain_ref, key_rot, key_normed, key_inverse, grad_key, grad_value,
):
    row, kv, step = pl.program_id(0), pl.program_id(1), pl.program_id(2)
    group_size = pl.num_programs(2) - 2
    cosine, sine = cos_ref[...], sin_ref[...]
    factor = 1.0 / math.sqrt(q_ref.shape[-1])

    @pl.when((row == 0) & (kv == 0) & (step == 0))
    def _():
        qgain_ref[...] = jnp.zeros_like(qgain_ref)
        kgain_ref[...] = jnp.zeros_like(kgain_ref)

    @pl.when(step == 0)
    def _():
        inverse, normed, rotated = normed_turned(k_ref[...], kg_ref[...], cosine, sine)
        key_rot[...] = rotated
        key_normed[...] = normed
        key_inverse[...] = jnp.broadcast_to(inverse, key_inverse.shape)
        grad_key[...] = jnp.zeros_like(grad_key)
        grad_value[...] = jnp.zeros_like(grad_value)

    @pl.when(step < group_size)
    def _():
        inverse, normed, query_rot = normed_turned(q_ref[...], qg_ref[...], cosine, sine)
        weights = weights_of(query_rot, key_rot[...], bias_ref[...])
        grad_out = go_ref[...]
        grad_value[...] += mm(weights.astype(BF16), grad_out, ((0,), (0,)))
        grad_weights = mm(grad_out, v_ref[...].astype(BF16), ((1,), (1,)))
        delta = jnp.sum(att_ref[...].astype(F32) * grad_out.astype(F32), axis=-1, keepdims=True)
        grad_scores = (weights * (grad_weights - delta) * factor).astype(BF16)
        grad_query = turn_back(mm(grad_scores, key_rot[...]), cosine, sine)
        grad_key[...] += mm(grad_scores, query_rot, ((0,), (0,)))
        qgain_ref[...] += jnp.sum(grad_query * normed, axis=0, keepdims=True)
        grad_ref[...] = norm_backward(grad_query, qg_ref[...], normed, inverse).astype(BF16)

    @pl.when(step == group_size)
    def _():
        grad = turn_back(grad_key[...], cosine, sine)
        normed = key_normed[...]
        kgain_ref[...] += jnp.sum(grad * normed, axis=0, keepdims=True)
        grad_ref[...] = norm_backward(
            grad, kg_ref[...], normed, key_inverse[...][:, :1]
        ).astype(BF16)

    @pl.when(step == group_size + 1)
    def _():
        grad_ref[...] = grad_value[...].astype(BF16)


def attention_specs(length, head_size, heads, kv_heads):
    group_size = heads // kv_heads

    def head(r, kv, g):
        return (r, kv * group_size + jnp.minimum(g, group_size - 1))

    block = (length, head_size)
    full = pl.BlockSpec((1, head_size), lambda r, kv, g: (0, 0))
    return head, [
        pl.BlockSpec(block, head),
        pl.BlockSpec(block, lambda r, kv, g: (r, heads + kv)),
        pl.BlockSpec(block, lambda r, kv, g: (r, heads + kv_heads + kv)),
        pl.BlockSpec(block, lambda r, kv, g: (r, 0)),
        pl.BlockSpec(block, lambda r, kv, g: (r, 0)),
        pl.BlockSpec((None, length, length), lambda r, kv, g: (r, 0, 0)),
        full,
        full,
    ]


def attend(pre, tables, gains, rows, heads, kv_heads):
    length, head_size = pre.shape[0] // rows, gains[0].shape[1]
    head, specs = attention_specs(length, head_size, heads, kv_heads)
    cost = rows * heads * length * length
    return pl.pallas_call(
        attend_kernel,
        grid=(rows, kv_heads, heads // kv_heads),
        in_specs=specs,
        out_specs=pl.BlockSpec((length, head_size), head),
        out_shape=jax.ShapeDtypeStruct((pre.shape[0], heads * head_size), BF16),
        scratch_shapes=[pltpu.VMEM((length, head_size), BF16)],
        cost_estimate=pl.CostEstimate(
            flops=4 * cost * head_size, bytes_accessed=6 * pre.size, transcendentals=cost
        ),
        name="attend",
    )(pre, pre, pre, *tables, *gains)


def attend_back(pre, tables, gains, attended, grad_attended, rows, heads, kv_heads):
    length, head_size = pre.shape[0] // rows, gains[0].shape[1]
    group_size = heads // kv_heads
    head, specs = attention_specs(length, head_size, heads, kv_heads)

    def target(r, kv, g):
        own = kv * group_size + g
        return (r, jnp.where(g < group_size, own, heads + kv + jnp.where(g > group_size, kv_heads, 0)))

    block = pl.BlockSpec((length, head_size), head)
    full = pl.BlockSpec((1, head_size), lambda r, kv, g: (0, 0))
    gain = jax.ShapeDtypeStruct((1, head_size), F32)
    cost = rows * heads * length * length
    wide = pltpu.VMEM((length, head_size), F32)
    return pl.pallas_call(
        attend_back_kernel,
        grid=(rows, kv_heads, group_size + 2),
        in_specs=specs + [block, block],
        out_specs=[pl.BlockSpec((length, head_size), target), full, full],
        out_shape=[jax.ShapeDtypeStruct(pre.shape, BF16), gain, gain],
        scratch_shapes=[pltpu.VMEM((length, head_size), BF16), wide, wide, wide, wide],
        cost_estimate=pl.CostEstimate(
            flops=10 * cost * head_size, bytes_accessed=10 * pre.size, transcendentals=cost
        ),
        name="attend_back",
    )(pre, pre, pre, *tables, *gains, attended, grad_attended)


TILE = 256
PACK = 16
GRANT = 60 * 1024 * 1024
HELD = 20 * 1024 * 1024


def pick_kernel(tiles, first, last, places_ref, *refs):
    e, j = pl.program_id(1), pl.program_id(2)
    third = len(refs) // 3
    sources, outs, totals = refs[:third], refs[third : 2 * third], refs[2 * third :]

    @pl.when(j < tiles[e])
    def _():
        for total in totals:
            total[...] = jnp.zeros_like(total)
        at = e * pl.num_programs(2) + j
        wanted = j * TILE + lax.broadcasted_iota(jnp.int32, (TILE, places_ref.shape[2]), 0)

        def add(g, carry):
            hits = jnp.where(places_ref[g] == wanted, 1.0, 0.0).astype(BF16)
            for source, total in zip(sources, totals):
                total[...] += mm(hits, source[g])
            return carry

        lax.fori_loop(first[at], last[at] + 1, add, 0)
        for out, total in zip(outs, totals):
            out[...] = total[...].astype(BF16)

    @pl.when(j >= tiles[e])
    def _():
        for out in outs:
            out[...] = jnp.zeros_like(out)


def pick(plan, source, width):
    experts, nodes, _, tokens = plan["places"].shape
    count = plan["tile_count"]
    cuts = 1
    while 2 * nodes * tokens * (width // cuts) > HELD and width % (256 * cuts) == 0:
        cuts *= 2
    part = width // cuts
    more = source.shape[2] - width
    out_specs = [pl.BlockSpec((None, TILE, part), lambda c, e, j, *_: (e, j, c))]
    in_specs = [
        pl.BlockSpec((None, nodes, 1, tokens), lambda c, e, j, *_: (e, 0, 0, 0)),
        pl.BlockSpec(
            (nodes, tokens, part), lambda c, e, j, *_: (0, 0, c), pipeline_mode=pl.Buffered(1)
        ),
    ]
    widths = [width]
    scratch = [pltpu.VMEM((TILE, part), F32)]
    if more:
        out_specs.append(pl.BlockSpec((None, TILE, more), lambda c, e, j, *_: (e, j, 0)))
        in_specs.append(
            pl.BlockSpec(
                (nodes, tokens, more),
                lambda c, e, j, *_: (0, 0, width // more),
                pipeline_mode=pl.Buffered(1),
            )
        )
        widths.append(more)
        scratch.append(pltpu.VMEM((TILE, more), F32))
    return pl.pallas_call(
        pick_kernel,
        grid_spec=pltpu.PrefetchScalarGridSpec(
            num_scalar_prefetch=3,
            grid=(cuts, experts, count),
            in_specs=in_specs,
            out_specs=out_specs,
            scratch_shapes=scratch,
        ),
        out_shape=[jax.ShapeDtypeStruct((experts, count * TILE, w), BF16) for w in widths],
        compiler_params=pltpu.CompilerParams(vmem_limit_bytes=GRANT),
        cost_estimate=pl.CostEstimate(
            flops=6 * experts * count * TILE * tokens * width,
            bytes_accessed=2 * nodes * tokens * width + 2 * experts * count * TILE * width,
            transcendentals=0,
        ),
        name="pick",
    )(
        plan["tiles"], plan["first"], plan["last"], plan["places"], *([source] * len(widths))
    )


def weight_kernel(tiles, left_ref, right_ref, own_ref, far_ref, total, *, axis, piece, group):
    e, j = pl.program_id(0), pl.program_id(1)

    @pl.when(j == 0)
    def _():
        total[...] = jnp.zeros_like(total)

    @pl.when(j * group < tiles[e])
    def _():
        total[...] += mm(left_ref[...], right_ref[...], ((0,), (0,)))

    @pl.when(j == pl.num_programs(1) - 1)
    def _():
        if axis == 0:
            own_ref[...] = total[:piece, :]
            far_ref[...] = total[piece:, :].astype(BF16)
        else:
            own_ref[...] = total[:, :piece]
            far_ref[...] = total[:, piece:].astype(BF16)


def weight_grad(plan, left, right, axis, piece):
    experts, height, deep = left.shape
    wide = right.shape[2]
    group = 2 if plan["tile_count"] % 2 == 0 else 1
    size = group * TILE

    def block(rows, columns):
        return pl.BlockSpec((None, rows, columns), lambda e, j, *_: (e, 0, 0))

    own = (piece, wide) if axis == 0 else (deep, piece)
    far = (deep - piece, wide) if axis == 0 else (deep, wide - piece)

    def rows_at(e, j, tiles):
        used = (tiles[e] + group - 1) // group
        return (e, jnp.minimum(j, jnp.maximum(used - 1, 0)), 0)

    return pl.pallas_call(
        functools.partial(weight_kernel, axis=axis, piece=piece, group=group),
        grid_spec=pltpu.PrefetchScalarGridSpec(
            num_scalar_prefetch=1,
            grid=(experts, height // size),
            in_specs=[
                pl.BlockSpec((None, size, deep), rows_at),
                pl.BlockSpec((None, size, wide), rows_at),
            ],
            out_specs=[block(*own), block(*far)],
            scratch_shapes=[pltpu.VMEM((deep, wide), F32)],
        ),
        out_shape=[
            jax.ShapeDtypeStruct((experts,) + own, F32),
            jax.ShapeDtypeStruct((experts,) + far, BF16),
        ],
        compiler_params=pltpu.CompilerParams(vmem_limit_bytes=GRANT),
        cost_estimate=pl.CostEstimate(
            flops=experts * height * deep * wide,
            bytes_accessed=experts * (height * (deep + wide) + 6 * deep * wide),
            transcendentals=0,
        ),
        name="weight_grad",
    )(plan["tiles"], left, right)


def expert_kernel(
    tiles, base, arrived_ref, extra_ref, cots_ref, gate_ref, up_ref, down_ref,
    weighed_ref, grad_gate_ref, grad_up_ref, produced_ref, back_ref, column_ref, *, expert_count,
):
    e, j = pl.program_id(0), pl.program_id(1)

    @pl.when(j < tiles[e])
    def _():
        lane = lax.broadcasted_iota(jnp.int32, extra_ref.shape, 1)
        own = base[0] + e
        gates = jnp.where(
            (lane == own) | (lane == own + expert_count), extra_ref[...].astype(F32), 0.0
        )
        gate_here = jnp.sum(gates, axis=-1, keepdims=True)
        gate_pre = mm(arrived_ref[...], gate_ref[...])
        up_pre = mm(arrived_ref[...], up_ref[...])
        grad_plain = mm(cots_ref[...], down_ref[...], ((1,), (1,)))
        sigmoid_gate = 1.0 / (1.0 + jnp.exp(-gate_pre))
        activated = gate_pre * sigmoid_gate
        hidden = activated * up_pre
        column = jnp.sum(hidden * grad_plain, axis=-1, keepdims=True)
        high = column.astype(BF16).astype(F32)
        spot = lax.broadcasted_iota(jnp.int32, column_ref.shape, 1)
        column_ref[...] = jnp.where(
            spot == 2 * e, high, jnp.where(spot == 2 * e + 1, column - high, 0.0)
        ).astype(BF16)
        weighed = (hidden * gate_here).astype(BF16)
        weighed_ref[...] = weighed
        grad_hidden = grad_plain * gate_here
        grad_gate = (
            grad_hidden * up_pre * sigmoid_gate * (1.0 + gate_pre * (1.0 - sigmoid_gate))
        ).astype(BF16)
        grad_up = (grad_hidden * activated).astype(BF16)
        grad_gate_ref[...] = grad_gate
        grad_up_ref[...] = grad_up
        produced_ref[...] = mm(weighed, down_ref[...]).astype(BF16)
        back_ref[...] = (
            mm(grad_gate, gate_ref[...], ((1,), (1,))) + mm(grad_up, up_ref[...], ((1,), (1,)))
        ).astype(BF16)

    @pl.when(j >= tiles[e])
    def _():
        for ref in (weighed_ref, grad_gate_ref, grad_up_ref, produced_ref, back_ref, column_ref):
            ref[...] = jnp.zeros_like(ref)


def run_experts(plan, base, arrived, extra, cots, gate, up, down, expert_count):
    experts, height, width = arrived.shape
    hidden = gate.shape[2]
    count = plan["tile_count"]

    def tile(size):
        return pl.BlockSpec((None, TILE, size), lambda e, j, *_: (e, j, 0))

    def whole(shape):
        return pl.BlockSpec((None,) + shape, lambda e, j, *_: (e, 0, 0))

    def out(size):
        return jax.ShapeDtypeStruct((experts, height, size), BF16)

    return pl.pallas_call(
        functools.partial(expert_kernel, expert_count=expert_count),
        grid_spec=pltpu.PrefetchScalarGridSpec(
            num_scalar_prefetch=2,
            grid=(experts, count),
            in_specs=[
                tile(width), tile(extra.shape[2]), tile(width),
                whole((width, hidden)), whole((width, hidden)), whole((hidden, width)),
            ],
            out_specs=[tile(hidden)] * 3 + [tile(width)] * 2 + [tile(128)],
        ),
        out_shape=[out(hidden)] * 3 + [out(width)] * 2 + [out(128)],
        compiler_params=pltpu.CompilerParams(vmem_limit_bytes=GRANT),
        cost_estimate=pl.CostEstimate(
            flops=6 * experts * height * width * hidden,
            bytes_accessed=2 * experts * (4 * height * width + 3 * height * hidden),
            transcendentals=experts * height * hidden // 2,
        ),
        name="run_experts",
    )(plan["tiles"], base, arrived, extra, cots, gate, up, down)


def spread_kernel(starts, places_ref, *refs):
    g = pl.program_id(0)
    half = len(refs) // 2
    experts, nodes = places_ref.shape[0], pl.num_programs(0)
    window = refs[-1]
    size = window.shape[0]
    totals = [None] * half
    for e in range(experts):
        start = pl.multiple_of(starts[e * nodes + g], PACK)
        wanted = start + lax.broadcasted_iota(jnp.int32, (size, places_ref.shape[2]), 0)
        hits = jnp.where(places_ref[e] == wanted, 1.0, 0.0).astype(BF16)
        for i in range(half):
            part = mm(hits, refs[i][e, pl.ds(start, size), :], ((0,), (0,)))
            totals[i] = part if totals[i] is None else totals[i] + part
    for i in range(half):
        refs[half + i][...] = totals[i].astype(BF16)


def spread(plan, sources):
    experts, nodes, _, tokens = plan["places"].shape
    window = plan["window"]
    return pl.pallas_call(
        spread_kernel,
        grid_spec=pltpu.PrefetchScalarGridSpec(
            num_scalar_prefetch=1,
            grid=(nodes,),
            in_specs=[pl.BlockSpec((experts, None, 1, tokens), lambda g, *_: (0, g, 0, 0))]
            + [
                pl.BlockSpec(source.shape, lambda g, *_: (0, 0, 0), pipeline_mode=pl.Buffered(1))
                for source in sources
            ],
            out_specs=[
                pl.BlockSpec((None, tokens, source.shape[2]), lambda g, *_: (g, 0, 0))
                for source in sources
            ],
            scratch_shapes=[pltpu.VMEM((window, 128), BF16)],
        ),
        out_shape=[
            jax.ShapeDtypeStruct((nodes, tokens, source.shape[2]), BF16) for source in sources
        ],
        compiler_params=pltpu.CompilerParams(vmem_limit_bytes=GRANT),
        cost_estimate=pl.CostEstimate(
            flops=2 * experts * nodes * tokens * window * sum(s.shape[2] for s in sources),
            bytes_accessed=sum(4 * s.size for s in sources),
            transcendentals=0,
        ),
        name="spread",
    )(plan["starts"], plan["places"], *sources)


def plan_places(member, slot, places):
    nodes, _, _ = member.shape
    counts = jnp.sum(member.astype(jnp.int32), axis=2)
    earlier = jnp.arange(nodes)[:, None] > jnp.arange(nodes)[None, :]
    offset = jnp.sum(jnp.where(earlier[:, :, None], counts[None], 0), axis=1)
    totals = jnp.sum(counts, axis=0)
    count = -(-(nodes * places) // TILE)
    edges = jnp.arange(count, dtype=jnp.int32) * TILE
    ends = offset + counts
    first = jnp.sum((ends[:, :, None] <= edges).astype(jnp.int32), axis=0)
    last = jnp.sum((offset[:, :, None] < edges + TILE).astype(jnp.int32), axis=0) - 1
    window = -(-places // PACK) * PACK + PACK
    window = min(window, count * TILE)
    starts = jnp.minimum(offset // PACK * PACK, count * TILE - window)
    packed = jnp.where(member, offset[:, :, None] + slot, -1)
    return {
        "places": jnp.moveaxis(packed, 1, 0)[:, :, None, :],
        "tiles": (totals + TILE - 1) // TILE,
        "first": jnp.minimum(first, nodes - 1).reshape(-1),
        "last": jnp.minimum(last, nodes - 1).reshape(-1),
        "starts": starts.T.reshape(-1),
        "tile_count": count,
        "window": window,
    }


def layer(
    layer_input,
    attention_gain,
    query_gain,
    key_gain,
    query_weight,
    key_weight,
    value_weight,
    output_weight,
    router_weight,
    expert_gain,
    gate_weight,
    up_weight,
    down_weight,
    routes,
    segments,
    cotangent,
):
    rows, local_length, model_width = layer_input.shape
    length = segments.shape[1]
    head_size = query_gain.shape[0]
    expert_count = router_weight.shape[1]
    local_experts, _, half_hidden = gate_weight.shape
    top_count = routes.shape[2]
    nodes = lax.axis_size("fsdp")
    tp_size = lax.axis_size("tp")
    node = lax.axis_index("fsdp")
    part = lax.axis_index("tp")
    heads = query_weight.shape[1] // head_size
    kv_heads = key_weight.shape[1] // head_size
    capacity = max(2, rows * length * top_count * 5 // (4 * expert_count))
    tokens = rows * local_length
    places = min(capacity, tokens)
    every = tp_size * tokens

    qkv_full = lax.all_gather(
        jnp.concatenate([query_weight, key_weight, value_weight], axis=1), "fsdp", axis=0, tiled=True
    )
    input_wide = layer_input.astype(F32)
    inverse_one = inverse_rms(input_wide)
    normed_one = input_wide * inverse_one
    normed_low = (normed_one * attention_gain).astype(BF16)
    normed_rows = gather_tp(normed_low, 1).reshape(every, model_width)
    output_full = lax.all_gather(output_weight, "fsdp", axis=0, tiled=True)
    router_full = lax.all_gather(router_weight, "fsdp", axis=0, tiled=True)

    places_in = jnp.concatenate(
        [
            ((part + j) % tp_size) * local_length + jnp.arange(local_length, dtype=jnp.int32)
            for j in range(tp_size)
        ]
    )
    doubled = jnp.concatenate([segments, segments], axis=1)
    ids = lax.dynamic_slice_in_dim(doubled, part * local_length, length, axis=1)
    starts = jnp.sum((segments[:, None, :] < ids[:, :, None]).astype(jnp.int32), axis=2)
    half_size = head_size // 2
    frequency = jnp.exp(jnp.arange(half_size, dtype=F32) * (-2.0 * math.log(ROPE_BASE) / head_size))
    angles = (places_in[None, :] - starts).astype(F32)[:, :, None] * frequency
    cosine, sine = jnp.cos(angles), jnp.sin(angles)
    cosine_table = jnp.concatenate([cosine, cosine], axis=-1).reshape(every, head_size)
    sine_table = jnp.concatenate([-sine, sine], axis=-1).reshape(every, head_size)
    allowed = (ids[:, :, None] == ids[:, None, :]) & (places_in[None, :] <= places_in[:, None])[None]
    tables = (cosine_table, sine_table, jnp.where(allowed, 0.0, NEGATIVE).astype(F32))
    gains = (query_gain.reshape(1, head_size), key_gain.reshape(1, head_size))

    gate_weight, up_weight, down_weight, normed_rows = lax.optimization_barrier(
        (gate_weight, up_weight, down_weight, normed_rows)
    )
    gate_full = gather_tp(gate_weight, 2)
    up_full = gather_tp(up_weight, 2)

    own_routes = lax.dynamic_slice_in_dim(routes, part * local_length, local_length, axis=1)
    own_routes = own_routes.reshape(tokens, top_count)
    all_routes = lax.all_gather(own_routes, "fsdp", axis=0).reshape(nodes, tokens, top_count)
    own_experts = node * local_experts + jnp.arange(local_experts, dtype=jnp.int32)
    member = jnp.any(all_routes[:, None, :, :] == own_experts[None, :, None, None], axis=-1)
    before = jnp.arange(tokens)[:, None] < jnp.arange(tokens)[None, :]
    slot = jnp.einsum(
        "get,tu->geu", member.astype(BF16), before.astype(BF16), preferred_element_type=F32
    ).astype(jnp.int32)
    plan = plan_places(member, slot, places)
    base = (node * local_experts).reshape(1).astype(jnp.int32)

    steady = {key: plan[key] for key in ("places", "tiles", "first", "last", "starts")}
    normed_rows, router_full, steady = lax.optimization_barrier((normed_rows, router_full, steady))
    plan = {**plan, **steady}
    pre = mm(normed_rows, qkv_full)
    cot_low = cotangent.reshape(tokens, model_width)
    cot_low, pre = lax.optimization_barrier((cot_low, pre))
    attended = attend(pre, tables, gains, rows, heads, kv_heads)
    made = {}

    def project(moving):
        held, moving = lax.optimization_barrier((attended, moving))
        projected = mm(held, output_full, ((1,), (1,)))
        projected = projected.reshape(rows, tp_size, local_length, model_width)
        made["middle"] = input_wide + scatter_tp([projected[:, j] for j in range(tp_size)])
        return moving

    def settle(moving):
        made["middle"], moving = lax.optimization_barrier((made["middle"], moving))
        return moving

    cot_all = ring_gather(cot_low, (project, settle))
    middle, down_weight = lax.optimization_barrier((made["middle"], down_weight))
    down_full = gather_tp(down_weight, 1)
    inverse_two = inverse_rms(middle)
    normed_two = middle * inverse_two
    expert_low = (normed_two * expert_gain).astype(BF16).reshape(tokens, model_width)

    logits = mm(expert_low, router_full)
    chosen = jnp.any(
        own_routes[:, :, None] == jnp.arange(expert_count, dtype=jnp.int32), axis=1
    )
    top = jnp.max(jnp.where(chosen, logits, NEGATIVE), axis=-1, keepdims=True)
    powers = jnp.where(chosen, jnp.exp(jnp.minimum(logits - top, 0.0)), 0.0)
    gates = powers / jnp.sum(powers, axis=-1, keepdims=True)
    high = lax.reduce_precision(gates, 8, 7)
    filler = jnp.zeros((tokens, -2 * expert_count % 128), BF16)
    sent = jnp.concatenate(
        [expert_low, high.astype(BF16), (gates - high).astype(BF16), filler], axis=1
    )
    rows_all = lax.all_gather(sent, "fsdp", axis=0)

    arrived, extra = pick(plan, rows_all, model_width)
    cots = pick(plan, cot_all, model_width)[0]
    weighed, grad_gate_pre, grad_up_pre, produced, back, columns = run_experts(
        plan, base, arrived, extra, cots, gate_full, up_full, down_full, expert_count
    )
    out_total = spread(plan, [produced])[0]
    out_total, back = lax.optimization_barrier((out_total, back))
    grad_total, columns = spread(plan, [back, columns])
    pairs = columns[:, :, : 2 * local_experts].astype(F32).reshape(nodes, tokens, local_experts, 2)
    column = jnp.sum(pairs, axis=-1)
    grad_gate = lax.all_to_all(column, "fsdp", split_axis=0, concat_axis=0, tiled=True)
    grad_gate = jnp.moveaxis(grad_gate, 0, 1).reshape(tokens, expert_count)
    weighed, grad_gate = lax.optimization_barrier((weighed, grad_gate))
    own_grads, far_grads = zip(
        weight_grad(plan, arrived, grad_gate_pre, 1, half_hidden),
        weight_grad(plan, arrived, grad_up_pre, 1, half_hidden),
        weight_grad(plan, weighed, cots, 0, half_hidden),
    )

    def send_far(kind):
        axis = 2 if kind < 2 else 1
        return [
            lax.ppermute(
                lax.slice_in_dim(
                    far_grads[kind], (j - 1) * half_hidden, j * half_hidden, axis=axis
                ),
                "tp",
                [(s, (s + j) % tp_size) for s in range(tp_size)],
            )
            for j in range(1, tp_size)
        ]

    moved = [send_far(0)]
    grad_rows = ring_scatter(grad_total)
    grad_rows, far_grads = lax.optimization_barrier((grad_rows, far_grads))
    moved += [send_far(kind) for kind in (1, 2)]
    expert_part = lax.psum_scatter(out_total, "fsdp", scatter_dimension=0, tiled=True)
    grad_logits = (
        gates * (grad_gate - jnp.sum(gates * grad_gate, axis=-1, keepdims=True))
    ).astype(BF16)
    router_part = mm(expert_low, grad_logits, ((0,), (0,)))
    grad_two = grad_rows.reshape(tokens, model_width).astype(F32) + mm(
        grad_logits, router_full, ((1,), (1,))
    )
    grad_two = grad_two.reshape(middle.shape)
    expert_gain_part = jnp.sum(grad_two * normed_two, axis=(0, 1))
    grad_middle = cotangent.astype(F32) + norm_backward(grad_two, expert_gain, normed_two, inverse_two)

    grad_low = gather_tp(grad_middle.astype(BF16), 1)
    grad_flat = grad_low.reshape(every, model_width)
    grad_attended = mm(grad_flat, output_full).astype(BF16)
    output_low = mm(grad_flat, attended, ((0,), (0,))).astype(BF16)
    output_low, grad_attended, expert_part = lax.optimization_barrier(
        (output_low, grad_attended, expert_part)
    )
    output_part = lax.psum_scatter(output_low, "fsdp", scatter_dimension=0, tiled=True)
    grad_pre, query_gain_part, key_gain_part = attend_back(
        pre, tables, gains, attended, grad_attended, rows, heads, kv_heads
    )
    qkv_low = mm(normed_rows, grad_pre, ((0,), (0,))).astype(BF16)
    qkv_grad = ring_scatter(qkv_low.reshape(nodes, -1, qkv_low.shape[1]))
    qkv_grad = qkv_grad.reshape(query_weight.shape[0], -1)
    grad_normed = mm(grad_pre, qkv_full, ((1,), (1,))).reshape(rows, tp_size, local_length, model_width)
    received = [
        lax.ppermute(
            grad_normed[:, j].astype(BF16), "tp", [(s, (s + j) % tp_size) for s in range(tp_size)]
        )
        for j in range(1, tp_size)
    ]

    moved, received, qkv_grad = lax.optimization_barrier((moved, received, qkv_grad))
    grad_one = grad_normed[:, 0]
    for value in received:
        grad_one = grad_one + value.astype(F32)
    attention_gain_part = jnp.sum(grad_one * normed_one, axis=(0, 1))
    input_grad = grad_middle + norm_backward(grad_one, attention_gain, normed_one, inverse_one)
    weight_grads = []
    for kind in range(3):
        total = own_grads[kind]
        for value in moved[kind]:
            total = total + value.astype(F32)
        weight_grads.append(total)
    gate_grad, up_grad, down_grad = weight_grads
    query_width, key_width = query_weight.shape[1], key_weight.shape[1]
    query_grad = qkv_grad[:, :query_width]
    key_grad = qkv_grad[:, query_width : query_width + key_width]
    value_grad = qkv_grad[:, query_width + key_width :]

    layer_output = (middle + expert_part.reshape(middle.shape).astype(F32)).astype(BF16)
    output_grad = output_part.astype(F32)

    kept = [
        value.reshape(nodes, tp_size, -1)
        for value in (
            router_part,
            attention_gain_part,
            expert_gain_part,
            query_gain_part,
            key_gain_part,
        )
    ]
    sizes = [value.shape[2] for value in kept]
    shares = jnp.concatenate(kept, axis=2)
    shares = jnp.pad(shares, ((0, 0), (0, 0), (0, -shares.shape[2] % 128)))
    shares = lax.all_to_all(
        shares.reshape(nodes, tp_size, -1, 128), "fsdp", split_axis=0, concat_axis=0, tiled=True
    )
    shares = jnp.sum(shares, axis=0)
    mine = jnp.zeros(shares.shape[1:], F32)
    for j in range(tp_size):
        share = lax.dynamic_index_in_dim(shares, (part + j) % tp_size, 0, keepdims=False)
        if j > 0:
            share = lax.ppermute(share, "tp", [(s, (s + j) % tp_size) for s in range(tp_size)])
        mine = mine + share
    mine = mine.reshape(-1)
    small = []
    at = 0
    for size in sizes:
        small.append(mine[at : at + size])
        at += size
    router_grad = small[0].reshape(-1, expert_count)
    attention_gain_grad, expert_gain_grad, query_gain_grad, key_gain_grad = small[1:]
    return (
        layer_output,
        input_grad,
        attention_gain_grad,
        query_gain_grad,
        key_gain_grad,
        query_grad,
        key_grad,
        value_grad,
        output_grad,
        router_grad,
        expert_gain_grad,
        gate_grad,
        up_grad,
        down_grad,
    )


def solution(mesh):
    return jax.shard_map(
        layer,
        mesh=mesh,
        in_specs=(
            P("fsdp", "tp", None),
            P(),
            P(),
            P(),
            P("fsdp", "tp"),
            P("fsdp", "tp"),
            P("fsdp", "tp"),
            P("fsdp", "tp"),
            P("fsdp", None),
            P(),
            P("fsdp", None, "tp"),
            P("fsdp", None, "tp"),
            P("fsdp", "tp", None),
            P("fsdp", None, None),
            P("fsdp", None),
            P("fsdp", "tp", None),
        ),
        out_specs=(
            P("fsdp", "tp", None),
            P("fsdp", "tp", None),
            P(("fsdp", "tp")),
            P(("fsdp", "tp")),
            P(("fsdp", "tp")),
            P("fsdp", "tp"),
            P("fsdp", "tp"),
            P("fsdp", "tp"),
            P("fsdp", "tp"),
            P(("fsdp", "tp"), None),
            P(("fsdp", "tp")),
            P("fsdp", None, "tp"),
            P("fsdp", None, "tp"),
            P("fsdp", "tp", None),
        ),
        check_vma=False,
    )
```
